32 devices in a mesh: fsdp: 8 (over z, x), ctx: 4 (over y, core).
Axes of the slice: x: 2, y: 2, z: 4, core: 2. Of those that a mesh axis runs over, the one named last changes fastest.
Arguments:
- block_input: bfloat16 [4096, 1024], P(('fsdp', 'ctx')), may hold values from -6 to 6
- attn_gain: bfloat16 [1024], P('fsdp'), may hold values from 0.25 to 1.75
- query_proj: bfloat16 [1024, 1024], P('fsdp'), may hold values from -0.1875 to 0.1875
- key_proj: bfloat16 [1024, 512], P('fsdp'), may hold values from -0.1875 to 0.1875
- value_proj: bfloat16 [1024, 512], P('fsdp'), may hold values from -0.1875 to 0.1875
- qk_gain: bfloat16 [128], P('fsdp'), may hold values from 0.099609375 to 1.8984375
- out_proj: bfloat16 [1024, 1024], P('fsdp'), may hold values from -0.75 to 0.75
- ffn_gain: bfloat16 [1024], P('fsdp'), may hold values from 0.25 to 1.75
- gate_proj: bfloat16 [4608, 1024], P('fsdp'), may hold values from -0.1875 to 0.1875
- up_proj: bfloat16 [4608, 1024], P('fsdp'), may hold values from -0.1875 to 0.1875
- down_proj: bfloat16 [4608, 1024], P('fsdp'), may hold values from -0.09375 to 0.09375
- seg_lengths: int32 [8, 4], P('fsdp'), may hold values from 1 to 256, 512 in all within a row
- out_cotangent: bfloat16 [4096, 1024], P(('fsdp', 'ctx')), may hold values from -6 to 6
Outputs:
- block_output: bfloat16 [4096, 1024], P(('fsdp', 'ctx'))
- input_grad: float32 [4096, 1024], P(('fsdp', 'ctx'))
- attn_gain_grad: float32 [1024], P('fsdp')
- query_grad: float32 [1024, 1024], P(('fsdp', 'ctx'))
- key_grad: float32 [1024, 512], P(('fsdp', 'ctx'))
- value_grad: float32 [1024, 512], P(('fsdp', 'ctx'))
- qk_gain_grad: float32 [128], P('fsdp')
- out_proj_grad: float32 [1024, 1024], P(('fsdp', 'ctx'))
- ffn_gain_grad: float32 [1024], P('fsdp')
- gate_grad: float32 [4608, 1024], P(('fsdp', 'ctx'))
- up_grad: float32 [4608, 1024], P(('fsdp', 'ctx'))
- down_grad: float32 [4608, 1024], P(('fsdp', 'ctx'))
The draws below stay inside these ranges and needn't reach their ends.
Inputs may be any that keep to these rules, and one draw needn't show every extreme that they name: `seg_lengths`: each row holds the lengths of the 4 segments of one group; they sum to 512.
All inputs are finite; a program needn't handle non-finite values.
Results may differ from the reference program's by a relative error of at most 0.017.
Values may be sent and summed in bfloat16 or wider, within the bound.
A program may use at most 256 MiB of HBM per device.

```python
import math
import jax
import jax.numpy as jnp
import numpy as np
from jax import lax

D = 1024
H = 16
KVH = 8
HEAD = 64
FF = 4608
NSEG = 4
HD = 1024
KVD = 512
GROUP = 512
TOKENS = 4096
SEG_MOST = 256
N_FSDP = 8


def with_spikes(array, stream_key, source, target, blocks, factor):
    owner, partner = [(jnp.arange(array.shape[position]) // (array.shape[position] // blocks)).reshape([-1 if axis == position else 1 for axis in range(array.ndim)]) for position in (source, target)]
    chosen = jax.random.permutation(stream_key, blocks)[partner]
    strong = (owner == chosen) | (owner == (partner + blocks // 2) % blocks)
    return jnp.where(strong, factor * array, array)


def block_scale(rng, extent, cuts, smallest, largest):
    factor_of = 1.0
    for dim, parts in cuts:
        steps = jax.random.uniform(jax.random.fold_in(jax.random.fold_in(rng, 6), dim), (parts,), jnp.float32, smallest / len(cuts), largest / len(cuts))
        factor_of = factor_of * jnp.repeat(jnp.exp(steps), extent[dim] // parts).reshape((-1,) + (1,) * (len(extent) - 1 - dim))
    return factor_of


def split_up(count, total, bound, lean):
    portions = [(1 << 20) // math.isqrt(rank ** lean) + 1 for rank in range(2, count + 1)]
    spare, given = total - bound - (count - 1), [1] * (count - 1)
    while spare > 0:
        movable = [i for i in range(count - 1) if given[i] < bound]
        pool, remaining = sum([portions[i] for i in movable]), spare
        for i in movable:
            addition = min(bound - given[i], max(1, remaining * portions[i] // pool), spare)
            given[i] = given[i] + addition
            spare = spare - addition
    return np.array([bound] + given)


def uneven_parts(rng, number_of, total, limit, lean):
    if number_of == 2:
        one = jax.random.randint(rng, (), max(1, total - limit), min(limit, total - 1) + 1)
        return jnp.stack([one, total - one])
    sizes = jnp.asarray(split_up(number_of, total, limit, lean), jnp.int32)
    couples = (number_of - 1) // 2
    source_of, taker = sizes[1:1 + 2 * couples:2], sizes[2:2 + 2 * couples:2]
    margin = jnp.minimum(source_of - 1, limit - taker)
    passed = jax.random.randint(jax.random.fold_in(rng, 1), (couples,), 0, 1 << 20) % (margin + 1)
    sizes = sizes.at[1:1 + 2 * couples:2].set(source_of - passed).at[2:2 + 2 * couples:2].set(taker + passed)
    return sizes[jax.random.permutation(jax.random.fold_in(rng, 2), number_of)]


def normal_values(key, extent, spread, limit, shards=(), kind=jnp.bfloat16):
    entries = spread * jax.random.normal(key, extent, jnp.float32)
    if shards:
        entries = entries * block_scale(key, extent, shards, -0.22, 0.18)
    return jnp.clip(entries, -limit, limit).astype(kind)


def heavy_noise(own_key, dims, scale, limit, shards, heavy, kind=jnp.bfloat16):
    result = scale * jax.random.normal(own_key, dims, jnp.float32)
    if shards:
        result = result * block_scale(own_key, dims, shards, -0.22, 0.18)
    return jnp.clip(with_spikes(result, jax.random.fold_in(own_key, 3), *heavy), -limit, limit).astype(kind)


def setup_inputs(seed: int = 0) -> dict:
    streams_of = jax.random.split(jax.random.key(seed), 14)
    block_input = heavy_noise(streams_of[0], (TOKENS, D), 1.0, 6.0, ((0, 32),), (0, 1, 32, 2.75))
    attn_gain = jnp.clip(1.0 + 0.15 * jax.random.normal(streams_of[1], (D,), jnp.float32), 0.25, 1.75).astype(jnp.bfloat16)
    query_proj = normal_values(streams_of[2], (D, HD), D ** -0.5, 0.1875, ((0, 8),))
    key_proj = normal_values(streams_of[3], (D, KVD), D ** -0.5, 0.1875, ((0, 8),))
    value_proj = normal_values(streams_of[4], (D, KVD), D ** -0.5, 0.1875, ((0, 8),))
    qk_gain = jnp.clip(1.0 + 0.18 * jax.random.normal(streams_of[5], (2 * HEAD,), jnp.float32), 0.099609375, 1.8984375).astype(jnp.bfloat16)
    out_proj = normal_values(streams_of[6], (HD, D), (HD // 16) ** -0.5, 0.75, ((0, 8),))
    ffn_gain = jnp.clip(1.0 + 0.15 * jax.random.normal(streams_of[7], (D,), jnp.float32), 0.25, 1.75).astype(jnp.bfloat16)
    gate_proj = normal_values(streams_of[8], (FF, D), D ** -0.5, 0.1875, ((0, 8),))
    up_proj = normal_values(streams_of[9], (FF, D), D ** -0.5, 0.1875, ((0, 8),))
    down_proj = normal_values(streams_of[10], (FF, D), FF ** -0.5, 0.09375, ((0, 8),))
    seg_lengths = jax.vmap(lambda own: uneven_parts(own, NSEG, GROUP, SEG_MOST, 2))(jax.random.split(streams_of[11], N_FSDP)).reshape((N_FSDP, NSEG)).astype(jnp.int32)
    out_cotangent = normal_values(streams_of[12], (TOKENS, D), 1.0, 6.0, ((0, 32),))
    return dict(block_input=block_input, attn_gain=attn_gain, query_proj=query_proj, key_proj=key_proj, value_proj=value_proj, qk_gain=qk_gain, out_proj=out_proj, ffn_gain=ffn_gain, gate_proj=gate_proj, up_proj=up_proj, down_proj=down_proj, seg_lengths=seg_lengths, out_cotangent=out_cotangent)


epsilon = 1e-05
rope_base = 1000000.0
masked_score = -1e+30

def to_bf16(values):
    return lax.optimization_barrier(values.astype(jnp.bfloat16))

def rms_scale(values):
    return lax.rsqrt(lax.optimization_barrier(jnp.mean(values * values, axis=-1, keepdims=True)) + epsilon)

def norm_back(values, inv_rms, gain_vec, upstream):
    scaled_up = upstream * gain_vec
    return inv_rms * scaled_up - values * (inv_rms * inv_rms * inv_rms) * lax.optimization_barrier(jnp.mean(scaled_up * values, axis=-1, keepdims=True))

def segment_positions(lengths, token_count):
    seg_ends = jnp.cumsum(lengths).astype(jnp.int32)
    seg_starts = (seg_ends - lengths).astype(jnp.int32)
    token_index = jnp.arange(token_count, dtype=jnp.int32)
    segment = lax.optimization_barrier(jnp.sum((token_index[:, None] >= seg_ends[None, :]).astype(jnp.int32), axis=1))
    seg_begin = lax.optimization_barrier(jnp.max(jnp.where(token_index[:, None] >= seg_starts[None, :], seg_starts[None, :], 0), axis=1))
    return (segment.astype(jnp.int32), (token_index - seg_begin).astype(jnp.int32))

def rope_tables(positions, head_width):
    half_width = head_width // 2
    frequency = rope_base ** (-(jnp.arange(half_width, dtype=jnp.float32) * 2.0 / head_width))
    angle_all = positions.astype(jnp.float32)[:, None] * frequency[None, :]
    return (jnp.cos(angle_all), jnp.sin(angle_all))

def rotate(values, cos_tab, sine_tab):
    half_width = values.shape[-1] // 2
    front_half = values[..., :half_width]
    back_half = values[..., half_width:]
    cos_b = cos_tab[:, None, :]
    sin_b = sine_tab[:, None, :]
    return jnp.concatenate([front_half * cos_b - back_half * sin_b, back_half * cos_b + front_half * sin_b], axis=-1)

def unrotate(upstream, cos_tab, sine_tab):
    half_width = upstream.shape[-1] // 2
    front_half = upstream[..., :half_width]
    back_half = upstream[..., half_width:]
    cos_b = cos_tab[:, None, :]
    sin_b = sine_tab[:, None, :]
    return jnp.concatenate([front_half * cos_b + back_half * sin_b, back_half * cos_b - front_half * sin_b], axis=-1)

def dot_nn(left_mat, right_mat):
    return jnp.dot(left_mat, right_mat, preferred_element_type=jnp.float32)

def group_pass(weights, x_group, dy_group, lengths_group):
    gain_attn, proj_q, proj_k, proj_v, gain_pair, proj_o, gain_ffn, w_gate, w_up, w_down = weights
    token_count = x_group.shape[0]
    segment, positions = segment_positions(lengths_group, token_count)
    cos_tab, sine_tab = rope_tables(positions, HEAD)
    gain_query = gain_pair[:HEAD]
    gain_key = gain_pair[HEAD:]
    x_float = x_group.astype(jnp.float32)
    inv_one = rms_scale(x_float)
    normed = to_bf16(x_float * inv_one * gain_attn)
    queries = dot_nn(normed, proj_q).reshape(token_count, H, HEAD)
    keys_raw = dot_nn(normed, proj_k).reshape(token_count, KVH, HEAD)
    values_b = to_bf16(dot_nn(normed, proj_v)).reshape(token_count, KVH, HEAD)
    inv_query = rms_scale(queries)
    q_rot = to_bf16(rotate(queries * inv_query * gain_query, cos_tab, sine_tab))
    inv_key = rms_scale(keys_raw)
    k_rot = to_bf16(rotate(keys_raw * inv_key * gain_key, cos_tab, sine_tab))
    head_share = H // KVH
    k_wide = jnp.repeat(k_rot, head_share, axis=1).astype(jnp.float32)
    v_wide = jnp.repeat(values_b, head_share, axis=1).astype(jnp.float32)
    q_wide = q_rot.astype(jnp.float32)
    scale_att = HEAD ** (-0.5)
    token_index = jnp.arange(token_count, dtype=jnp.int32)
    allowed = (segment[:, None] == segment[None, :]) & (token_index[None, :] <= token_index[:, None])
    scores = jnp.einsum('qhd,khd->hqk', q_wide, k_wide) * scale_att
    scores = jnp.where(allowed[None], scores, masked_score)
    top_score = lax.optimization_barrier(jnp.max(scores, axis=2, keepdims=True))
    log_total = top_score + jnp.log(lax.optimization_barrier(jnp.sum(jnp.exp(scores - top_score), axis=2, keepdims=True)))
    prob_full = jnp.exp(scores - log_total)
    prob_wide = to_bf16(prob_full).astype(jnp.float32)
    attn_out = to_bf16(jnp.einsum('hqk,khd->qhd', prob_wide, v_wide))
    attn_flat = attn_out.reshape(token_count, H * HEAD)
    mixed_res = x_float + dot_nn(attn_flat, proj_o)
    inv_two = rms_scale(mixed_res)
    ffn_in = to_bf16(mixed_res * inv_two * gain_ffn)
    gate_pre = dot_nn(ffn_in, w_gate.T)
    up_pre = dot_nn(ffn_in, w_up.T)
    gate_sig = jax.nn.sigmoid(gate_pre)
    active = gate_pre * gate_sig
    hidden = to_bf16(active * up_pre)
    block_out = (mixed_res + dot_nn(hidden, w_down)).astype(jnp.bfloat16)
    dy_float = dy_group.astype(jnp.float32)
    d_hidden = dot_nn(dy_group, w_down.T)
    d_gate = to_bf16(d_hidden * up_pre * gate_sig * (1.0 + gate_pre * (1.0 - gate_sig)))
    d_up = to_bf16(d_hidden * active)
    grad_down = dot_nn(hidden.T, dy_group)
    grad_gate = dot_nn(d_gate.T, ffn_in)
    grad_up = dot_nn(d_up.T, ffn_in)
    d_ffn_in = dot_nn(d_gate, w_gate) + dot_nn(d_up, w_up)
    grad_gain_ffn = lax.optimization_barrier(jnp.sum(d_ffn_in * mixed_res * inv_two, axis=0))
    d_mixed = dy_float + norm_back(mixed_res, inv_two, gain_ffn, d_ffn_in)
    d_mixed_b = to_bf16(d_mixed)
    grad_o = dot_nn(attn_flat.T, d_mixed_b)
    d_attn = to_bf16(dot_nn(d_mixed_b, proj_o.T)).reshape(token_count, H, HEAD)
    d_attn_f = d_attn.astype(jnp.float32)
    row_delta = lax.optimization_barrier(jnp.sum(d_attn_f * attn_out.astype(jnp.float32), axis=2)).T[:, :, None]
    d_prob = jnp.einsum('qhd,khd->hqk', d_attn_f, v_wide)
    d_score = to_bf16(prob_full * (d_prob - row_delta) * scale_att).astype(jnp.float32)
    d_q_rot = to_bf16(jnp.einsum('hqk,khd->qhd', d_score, k_wide))
    d_k_wide = jnp.einsum('hqk,qhd->khd', d_score, q_wide)
    d_k_rot = to_bf16(lax.optimization_barrier(jnp.sum(d_k_wide.reshape(token_count, KVH, head_share, HEAD), axis=2)))
    d_v_wide = jnp.einsum('hqk,qhd->khd', prob_wide, d_attn_f)
    d_values = to_bf16(lax.optimization_barrier(jnp.sum(d_v_wide.reshape(token_count, KVH, head_share, HEAD), axis=2)))
    d_q_norm = unrotate(d_q_rot.astype(jnp.float32), cos_tab, sine_tab)
    d_k_norm = unrotate(d_k_rot.astype(jnp.float32), cos_tab, sine_tab)
    grad_gain_q = lax.optimization_barrier(jnp.sum(d_q_norm * queries * inv_query, axis=(0, 1)))
    grad_gain_k = lax.optimization_barrier(jnp.sum(d_k_norm * keys_raw * inv_key, axis=(0, 1)))
    d_queries = to_bf16(norm_back(queries, inv_query, gain_query, d_q_norm)).reshape(token_count, H * HEAD)
    d_keys = to_bf16(norm_back(keys_raw, inv_key, gain_key, d_k_norm)).reshape(token_count, KVH * HEAD)
    d_values_flat = d_values.reshape(token_count, KVH * HEAD)
    grad_q = dot_nn(normed.T, d_queries)
    grad_k = dot_nn(normed.T, d_keys)
    grad_v = dot_nn(normed.T, d_values_flat)
    d_normed = dot_nn(d_queries, proj_q.T) + dot_nn(d_keys, proj_k.T) + dot_nn(d_values_flat, proj_v.T)
    grad_gain_attn = lax.optimization_barrier(jnp.sum(d_normed * x_float * inv_one, axis=0))
    d_input = d_mixed + norm_back(x_float, inv_one, gain_attn, d_normed)
    grad_sums = (grad_gain_attn, grad_q, grad_k, grad_v, jnp.concatenate([grad_gain_q, grad_gain_k]), grad_o, grad_gain_ffn, grad_gate, grad_up, grad_down)
    return (block_out, d_input, grad_sums)

def reference(block_input, attn_gain, query_proj, key_proj, value_proj, qk_gain, out_proj, ffn_gain, gate_proj, up_proj, down_proj, seg_lengths, out_cotangent):
    weights = (attn_gain.astype(jnp.float32), query_proj, key_proj, value_proj, qk_gain.astype(jnp.float32), out_proj, ffn_gain.astype(jnp.float32), gate_proj, up_proj, down_proj)
    x_groups = block_input.reshape(N_FSDP, GROUP, D)
    dy_groups = out_cotangent.reshape(N_FSDP, GROUP, D)
    initial = jax.tree.map(lambda weight: jnp.zeros(weight.shape, jnp.float32), weights)

    def group_step(carried, inputs):
        x_group, dy_group, lengths_group = inputs
        out_group, dx_group, grad_sums = group_pass(weights, x_group, dy_group, lengths_group)
        summed = tuple((left_term + right_term for left_term, right_term in zip(carried, grad_sums)))
        return (summed, (out_group, dx_group))
    totals, (out_all, dx_all) = lax.scan(group_step, initial, (x_groups, dy_groups, seg_lengths))
    return (out_all.reshape(TOKENS, D), dx_all.reshape(TOKENS, D), totals[0], totals[1], totals[2], totals[3], totals[4], totals[5], totals[6], totals[7], totals[8], totals[9])
```

```python
import jax
import jax.numpy as jnp
from jax import lax
from jax.experimental import pallas as pl
from jax.experimental.pallas import tpu as pltpu
from jax.sharding import PartitionSpec as P

H = 16
KVH = 8
HEAD = 64


epsilon = 1e-05
rope_base = 1000000.0
masked_score = -1e30


def rms_scale(values):
    return lax.rsqrt(jnp.mean(values * values, axis=-1, keepdims=True) + epsilon)


def norm_back(values, inv_rms, gain_vec, upstream):
    scaled_up = upstream * gain_vec
    return inv_rms * scaled_up - values * (inv_rms * inv_rms * inv_rms) * jnp.mean(
        scaled_up * values, axis=-1, keepdims=True
    )


def segment_positions(lengths, token_count):
    seg_ends = jnp.cumsum(lengths)
    seg_starts = seg_ends - lengths
    token_index = jnp.arange(token_count, dtype=jnp.int32)
    segment = jnp.sum((token_index[:, None] >= seg_ends[None, :]).astype(jnp.int32), axis=1)
    seg_begin = jnp.max(
        jnp.where(token_index[:, None] >= seg_starts[None, :], seg_starts[None, :], 0), axis=1
    )
    return (segment, token_index - seg_begin)


def rope_tables(positions, head_width):
    half_width = head_width // 2
    frequency = rope_base ** (-(jnp.arange(half_width, dtype=jnp.float32) * 2.0 / head_width))
    angle_all = positions.astype(jnp.float32)[:, None] * frequency[None, :]
    return (jnp.cos(angle_all), jnp.sin(angle_all))


def rotate(values, cos_tab, sine_tab):
    half_width = values.shape[-1] // 2
    front_half = values[..., :half_width]
    back_half = values[..., half_width:]
    cos_b = cos_tab[:, None, :]
    sin_b = sine_tab[:, None, :]
    return jnp.concatenate(
        [front_half * cos_b - back_half * sin_b, back_half * cos_b + front_half * sin_b], axis=-1
    )


def unrotate(upstream, cos_tab, sine_tab):
    half_width = upstream.shape[-1] // 2
    front_half = upstream[..., :half_width]
    back_half = upstream[..., half_width:]
    cos_b = cos_tab[:, None, :]
    sin_b = sine_tab[:, None, :]
    return jnp.concatenate(
        [front_half * cos_b + back_half * sin_b, back_half * cos_b - front_half * sin_b], axis=-1
    )


def dot_nn(left_mat, right_mat):
    return jnp.dot(left_mat, right_mat, preferred_element_type=jnp.float32)


def dot_nt(left_mat, right_mat):
    return lax.dot_general(
        left_mat, right_mat, (((1,), (1,)), ((), ())), preferred_element_type=jnp.float32
    )


def dot_tn(left_mat, right_mat):
    return lax.dot_general(
        left_mat, right_mat, (((0,), (0,)), ((), ())), preferred_element_type=jnp.float32
    )


MESH = pl.DeviceIdType.MESH
BF = jnp.bfloat16
F32 = jnp.float32


def factor(name):
    count = lax.axis_size(name)
    if name == "ctx":
        direct = 2
    else:
        direct = 1
        while direct * direct * 4 <= count:
            direct *= 2
    return count // direct, direct


class Place:
    def __init__(self, name):
        self.name = name
        self.L, self.D = factor(name)
        index = lax.axis_index(name)
        self.l = index // self.D
        self.d = index % self.D

    def dev(self, l, d):
        return {self.name: l * self.D + d}

    def off(self, dd):
        return lax.rem(self.d + dd, self.D)


def remote(src, dst, ssem, rsem, dev):
    return pltpu.make_async_remote_copy(
        src_ref=src, dst_ref=dst, send_sem=ssem, recv_sem=rsem, device_id=dev, device_id_type=MESH
    )


def add_rows(dst, parts, lead):
    rows = dst.shape[-2]
    step = 16 if rows % 16 == 0 else rows

    def one(pick):
        def body(i, carry):
            at = pl.ds(pl.multiple_of(i * step, step), step) if step != rows else slice(None)
            if dst.dtype == BF and len(parts) == 2:
                pick(dst)[at, :] = pick(parts[0])[at, :] + pick(parts[1])[at, :]
                return carry
            total = pick(parts[0])[at, :].astype(F32)
            for part in parts[1:]:
                total = total + pick(part)[at, :].astype(F32)
            pick(dst)[at, :] = total.astype(dst.dtype)
            return carry

        if step == rows:
            body(0, 0)
        else:
            lax.fori_loop(0, rows // step, body, 0)

    if lead is None:
        one(lambda ref: ref)
    else:
        for j in range(lead):
            one(lambda ref, j=j: ref.at[j])


def line_neighbors(p, act):
    @pl.when(p.l > 0)
    def _():
        act(-1)

    @pl.when(p.l < p.L - 1)
    def _():
        act(1)


def pieces(rows, most):
    for count in range(most, 1, -1):
        if rows % (16 * count) == 0:
            return count
    return 1


def cut(first, rows, size):
    res = []
    while rows > 0:
        take = min(size, rows)
        res.append((first, take, "line"))
        first, rows = first + take, rows - take
    return res


class Gather:
    def __init__(self, name, shape, dtype, split):
        self.name, self.shape, self.dtype = name, shape, dtype
        self.L, self.D = factor(name)
        rows = shape[0]
        self.parts = []
        if split == "both":
            units = rows // 16
            lead = max(1, (units + 3) // 6)
            self.parts = [(0, lead * 16, "dir")] + cut(lead * 16, rows - lead * 16, 32)
        elif pieces(rows, 4) > 1:
            count = pieces(rows, 4)
            size = rows // count
            self.parts = [(i * size, size, split) for i in range(count)]
        else:
            self.parts = [(0, rows, split)]
        self.outs = [jax.ShapeDtypeStruct((self.L, self.D) + shape, dtype)]
        self.scratch = []
        dma = pltpu.SemaphoreType.DMA
        L, D = self.L, self.D
        for _, _, kind in self.parts:
            if kind == "line":
                self.scratch += [dma((2, L)), dma((L,)), dma((D, L)), dma((D, L))]
            else:
                self.scratch += [dma((D,)), dma((D,)), dma((D, 2, L)), dma((D, L))]

    def gens(self, p, ins, outs, scr):
        src, out = ins[0], outs[0]
        res = []
        for i, (r0, r, kind) in enumerate(self.parts):
            f = self.line_first if kind == "line" else self.dir_first
            res.append((0, f(p, src, out, r0, r, scr[4 * i : 4 * i + 4], i == 0)))
        return res

    def line_first(self, p, src, out, r0, r, sems, keep):
        ls, lr, ds, dr = sems
        L, D, l, d = p.L, p.D, p.l, p.d
        own = src.at[pl.ds(r0, r), :]

        def V(q, dd):
            return out.at[q, dd, pl.ds(r0, r), :]

        def line(q, dirn, view):
            return remote(view, V(q, d), ls.at[(dirn + 1) // 2, q], lr.at[q], p.dev(l + dirn, d))

        def direct(q, view, k):
            return remote(view, V(q, d), ds.at[k - 1, q], dr.at[k - 1, q], p.dev(l, p.off(k)))

        line_neighbors(p, lambda dirn: line(l, dirn, own).start())
        for k in range(1, D):
            direct(l, own, k).start()
        if keep:
            out[l, d] = src[...]
        yield
        for k in range(1, L):
            for sgn in (-1, 1):
                q = l + sgn * k

                @pl.when((q >= 0) & (q < L))
                def _(q=q, sgn=sgn):
                    line(q, -sgn, V(q, d)).wait_recv()
                    for m in range(1, D):
                        direct(q, V(q, d), m).start()

                    @pl.when((l - sgn >= 0) & (l - sgn < L))
                    def _():
                        line(q, -sgn, V(q, d)).start()

            yield
        for q in range(L):
            for k in range(1, D):
                w = V(q, p.off(D - k))
                remote(w, w, ds.at[k - 1, q], dr.at[k - 1, q], p.dev(l, p.off(k))).wait_recv()
        yield "drain"
        for q in range(L):
            for k in range(1, D):
                direct(q, V(q, d), k).wait_send()
        for k in range(0, L):
            for sgn in (-1, 1):
                if k == 0:
                    q = l

                    @pl.when((l - sgn >= 0) & (l - sgn < L))
                    def _(sgn=sgn):
                        line(l, -sgn, own).wait_send()
                else:
                    q = l + sgn * k

                    @pl.when((q >= 0) & (q < L) & (l - sgn >= 0) & (l - sgn < L))
                    def _(q=q, sgn=sgn):
                        line(q, -sgn, V(q, d)).wait_send()

    def dir_first(self, p, src, out, r0, r, sems, keep):
        ds, dr, ls, lr = sems
        L, D, l, d = p.L, p.D, p.l, p.d
        own = src.at[pl.ds(r0, r), :]

        def V(q, dd):
            return out.at[q, dd, pl.ds(r0, r), :]

        def line(j, q, dirn, view):
            return remote(
                view,
                V(q, p.off(D - j)),
                ls.at[j, (dirn + 1) // 2, q],
                lr.at[j, q],
                p.dev(l + dirn, d),
            )

        def direct(k):
            return remote(own, V(l, d), ds.at[k - 1], dr.at[k - 1], p.dev(l, p.off(k)))

        for k in range(1, D):
            direct(k).start()
        line_neighbors(p, lambda dirn: line(0, l, dirn, own).start())
        if keep:
            out[l, d] = src[...]
        yield
        for j in range(1, D):
            w = V(l, p.off(D - j))
            remote(w, w, ds.at[j - 1], dr.at[j - 1], p.dev(l, p.off(j))).wait_recv()
            line_neighbors(p, lambda dirn: line(j, l, dirn, w).start())
        yield
        for k in range(1, L):
            for j in range(D):
                for sgn in (-1, 1):
                    q = l + sgn * k

                    @pl.when((q >= 0) & (q < L))
                    def _(q=q, sgn=sgn, j=j):
                        w = V(q, p.off(D - j))
                        line(j, q, -sgn, w).wait_recv()

                        @pl.when((l - sgn >= 0) & (l - sgn < L))
                        def _():
                            line(j, q, -sgn, w).start()

            yield "drain" if k == L - 1 else None
        for k in range(1, D):
            direct(k).wait_send()
        for k in range(0, L):
            for j in range(D):
                for sgn in (-1, 1):
                    q = l + sgn * k if k else l

                    @pl.when((q >= 0) & (q < L) & (l - sgn >= 0) & (l - sgn < L))
                    def _(q=q, sgn=sgn, j=j):
                        line(j, q, -sgn, own if (k == 0 and j == 0) else V(q, p.off(D - j))).wait_send()


class Spread:
    def __init__(self, shape, dtype, chunks):
        self.shape, self.dtype, self.chunks = shape, dtype, chunks
        self.L, self.D = factor("fsdp")
        if lax.axis_size("ctx") != self.L:
            raise ValueError("unsupported mesh")
        self.name = "fsdp"
        self.outs = [jax.ShapeDtypeStruct((self.D,) + shape, dtype)]
        dma = pltpu.SemaphoreType.DMA
        self.scratch = [dma((chunks, 2)), dma((chunks,)), dma((chunks, self.D)), dma((chunks, self.D))]

    def gens(self, p, ins, outs, scr):
        rows = self.shape[0] // self.chunks
        return [(i, self.one(p, ins[0], outs[0], i, rows, scr)) for i in range(self.chunks)]

    def one(self, p, src, out, i, rows, scr):
        ls, lr, ds, dr = scr
        l, d, D = p.l, p.d, p.D
        c = lax.axis_index("ctx")
        own = src.at[pl.ds(i * rows, rows), :]
        at_home = l == c

        def V(dd):
            return out.at[dd, pl.ds(i * rows, rows), :]

        def line(dirn, view):
            return remote(view, V(d), ls.at[i, (dirn + 1) // 2], lr.at[i], p.dev(l + dirn, d))

        def direct(k, view):
            return remote(view, V(d), ds.at[i, k - 1], dr.at[i, k - 1], p.dev(l, p.off(k)))

        @pl.when(at_home)
        def _():
            line_neighbors(p, lambda dirn: line(dirn, own).start())
            for k in range(1, D):
                direct(k, own).start()
            if i == 0:
                out[d] = src[...]

        yield

        @pl.when(l > c)
        def _():
            line(1, V(d)).wait_recv()

            @pl.when(l < p.L - 1)
            def _():
                line(1, V(d)).start()

            for k in range(1, D):
                direct(k, V(d)).start()

        @pl.when(l < c)
        def _():
            line(-1, V(d)).wait_recv()

            @pl.when(l > 0)
            def _():
                line(-1, V(d)).start()

            for k in range(1, D):
                direct(k, V(d)).start()

        yield
        for k in range(1, D):
            w = V(p.off(D - k))
            remote(w, w, ds.at[i, k - 1], dr.at[i, k - 1], p.dev(l, p.off(k))).wait_recv()
        yield "drain"
        for k in range(1, D):
            direct(k, V(d)).wait_send()

        @pl.when((l <= c) & (l > 0))
        def _():
            line(-1, V(d)).wait_send()

        @pl.when((l >= c) & (l < p.L - 1))
        def _():
            line(1, V(d)).wait_send()


class Reduce:
    def __init__(self, name, shape, dtype, most=1, lines=0, first=0):
        self.name, self.shape, self.dtype, self.first = name, shape, dtype, first
        self.wait = 1 if name == "ctx" else 0
        self.L, self.D = factor(name)
        L, D = self.L, self.D
        self.outs = [jax.ShapeDtypeStruct(shape, F32)]
        dma = pltpu.SemaphoreType.DMA
        self.count = pieces(shape[0], most if L * D <= 8 else min(most, 4))
        unit = (shape[0] // self.count,) + shape[1:]
        self.scratch = []
        self.kinds = ["dir"] * (self.count - lines) + ["line"] * min(lines, self.count)
        for kind in self.kinds:
            if kind == "line":
                self.scratch += [
                    pltpu.VMEM((L, D) + unit, dtype),
                    pltpu.VMEM((L, D) + unit, dtype),
                    pltpu.VMEM((D,) + unit, dtype),
                    pltpu.VMEM((max(D - 1, 1),) + unit, dtype),
                    dma((2, L)),
                    dma((2, L)),
                    dma((D,)),
                    dma((D,)),
                ]
            else:
                self.scratch += [
                    pltpu.VMEM((L,) + unit, dtype),
                    pltpu.VMEM((L,) + unit, dtype),
                    pltpu.VMEM((L,) + unit, dtype),
                    pltpu.VMEM((max(D - 1, 1), L) + unit, dtype),
                    dma((2, L)),
                    dma((2, L)),
                    dma((D, L)),
                    dma((D, L)),
                ]

    def gens(self, p, ins, outs, scr):
        size = self.shape[0] // self.count
        res = []
        for i, kind in enumerate(self.kinds):
            at = pl.ds(i * size, size)
            f = self.line_first if kind == "line" else self.dir_first
            start = 0 if kind == "line" else self.first + i
            res.append((start, f(p, ins[0], outs[0].at[at, :], at, scr[8 * i : 8 * i + 8])))
        return res

    def line_sum(self, p, own, from_left, from_right, ls, lr, lead, prep):
        L, l = p.L, p.l

        def right(q, view):
            return remote(view, from_left.at[q], ls.at[1, q], lr.at[1, q], p.dev(l + 1, p.d))

        def left(q, view):
            return remote(view, from_right.at[q], ls.at[0, q], lr.at[0, q], p.dev(l - 1, p.d))

        for t in range(L):
            qr, ql = L - 1 - t, t
            prep(qr)
            if qr > 0:

                @pl.when(l == 0)
                def _():
                    right(qr, own(qr)).start()

            prep(ql)
            if ql < L - 1:

                @pl.when(l == L - 1)
                def _():
                    left(ql, own(ql)).start()

        yield
        for k in range(1, L - 1):

            @pl.when(l == k)
            def _():
                for q in range(L - 1, k, -1):
                    right(q, from_left.at[q]).wait_recv()
                    add_rows(from_left.at[q], [from_left.at[q], own(q)], lead)
                    right(q, from_left.at[q]).start()

            @pl.when(l == L - 1 - k)
            def _():
                for q in range(L - 1 - k):
                    left(q, from_right.at[q]).wait_recv()
                    add_rows(from_right.at[q], [from_right.at[q], own(q)], lead)
                    left(q, from_right.at[q]).start()

            yield

    def line_total(self, p, own, from_left, from_right, ls, lr, dst, lead):
        l, L = p.l, p.L

        def arrive(way):
            v = (from_left if way == 1 else from_right).at[l]
            remote(v, v, ls.at[way, l], lr.at[way, l], p.dev(l + 1 - 2 * way, p.d)).wait_recv()

        @pl.when(l == 0)
        def _():
            arrive(0)
            add_rows(dst, [own(l), from_right.at[l]], lead)

        @pl.when(l == L - 1)
        def _():
            arrive(1)
            add_rows(dst, [own(l), from_left.at[l]], lead)

        if L > 2:

            @pl.when((l > 0) & (l < L - 1))
            def _():
                arrive(0)
                arrive(1)
                add_rows(dst, [own(l), from_left.at[l], from_right.at[l]], lead)

    def line_drain(self, p, from_left, from_right, ls, lr):
        L, l = p.L, p.l
        for q in range(L):
            if q > 0:

                @pl.when(l < q)
                def _():
                    v = from_left.at[q]
                    remote(v, v, ls.at[1, q], lr.at[1, q], p.dev(l + 1, p.d)).wait_send()

            if q < L - 1:

                @pl.when(l > q)
                def _():
                    v = from_right.at[q]
                    remote(v, v, ls.at[0, q], lr.at[0, q], p.dev(l - 1, p.d)).wait_send()

    def line_first(self, p, src, out, at, scr):
        from_left, from_right, acc, box, ls, lr, ds, dr = scr
        D, l, d = p.D, p.l, p.d

        def own(q):
            return src.at[q, :, at, :]

        yield from self.line_sum(p, own, from_left, from_right, ls, lr, D, lambda q: None)
        self.line_total(p, own, from_left, from_right, ls, lr, acc, D)

        def direct(k):
            return remote(
                acc.at[p.off(k)], box.at[k - 1], ds.at[k - 1], dr.at[k - 1], p.dev(l, p.off(k))
            )

        for k in range(1, D):
            direct(k).start()
        yield "late"
        for k in range(1, D):
            direct(k).wait_recv()
        add_rows(out, [acc.at[d]] + [box.at[k - 1] for k in range(1, D)], None)
        yield "drain"
        for k in range(1, D):
            direct(k).wait_send()
        self.line_drain(p, from_left, from_right, ls, lr)

    def dir_first(self, p, src, out, at, scr):
        from_left, from_right, acc, box, ls, lr, ds, dr = scr
        L, D, l, d = p.L, p.D, p.l, p.d

        def direct(k, q):
            return remote(
                src.at[q, p.off(k), at, :],
                box.at[k - 1, q],
                ds.at[k - 1, q],
                dr.at[k - 1, q],
                p.dev(l, p.off(k)),
            )

        order = []
        for t in range(L):
            for q in (L - 1 - t, t):
                if q not in order:
                    order.append(q)
        for q in order:
            for k in range(1, D):
                direct(k, q).start()
        yield
        ready = set()

        def prep(q):
            if q in ready:
                return
            ready.add(q)
            for k in range(1, D):
                direct(k, q).wait_recv()
            add_rows(
                acc.at[q], [src.at[q, d, at, :]] + [box.at[k - 1, q] for k in range(1, D)], None
            )

        def own(q):
            return acc.at[q]

        yield from self.line_sum(p, own, from_left, from_right, ls, lr, None, prep)
        for _ in range(self.wait):
            yield
        self.line_total(p, own, from_left, from_right, ls, lr, out, None)
        yield "drain"
        for q in range(L):
            for k in range(1, D):
                direct(k, q).wait_send()
        self.line_drain(p, from_left, from_right, ls, lr)


def greet(places):
    barrier = pltpu.get_barrier_semaphore()
    count = 0
    for p in places:
        for k in range(1, p.D):
            pl.semaphore_signal(
                barrier, inc=1, device_id=p.dev(p.l, p.off(k)), device_id_type=MESH
            )
        count = count + (p.D - 1)
        line_neighbors(
            p,
            lambda dirn: pl.semaphore_signal(
                barrier, inc=1, device_id=p.dev(p.l + dirn, p.d), device_id_type=MESH
            ),
        )
        count = count + jnp.where(p.l > 0, 1, 0) + jnp.where(p.l < p.L - 1, 1, 0)
    pl.semaphore_wait(barrier, count)


def run_all(live):
    live = sorted(live, key=lambda pair: pair[0])
    for _, g in live:
        next(g)
    late, drains, slot = [], [], 0
    while live:
        rest = []
        for start, g in live:
            if start > slot:
                rest.append((start, g))
                continue
            mark = next(g)
            if mark == "drain":
                drains.append(g)
            elif mark == "late":
                late.append(g)
            else:
                rest.append((start, g))
        live, slot = rest, slot + 1
    for g in late:
        next(g)
    for g in late + drains:
        for _ in g:
            pass


def communicate(ops, arrays, cid):
    axes = sorted({op.name for op in ops})
    outs = [shape for op in ops for shape in op.outs]
    scratch = [s for op in ops for s in op.scratch]

    def kernel(*refs):
        ins = refs[: len(arrays)]
        out_refs = refs[len(arrays) : len(arrays) + len(outs)]
        scr = refs[len(arrays) + len(outs) :]
        places = {name: Place(name) for name in axes}
        greet([places[name] for name in axes])
        live = []
        o = s = 0
        for i, op in enumerate(ops):
            live += op.gens(
                places[op.name],
                [ins[i]],
                out_refs[o : o + len(op.outs)],
                scr[s : s + len(op.scratch)],
            )
            o += len(op.outs)
            s += len(op.scratch)
        run_all(live)

    vm = pl.BlockSpec(memory_space=pltpu.VMEM)
    return pl.pallas_call(
        kernel,
        out_shape=outs,
        in_specs=[vm] * len(arrays),
        out_specs=[vm] * len(outs),
        scratch_shapes=scratch,
        compiler_params=pltpu.CompilerParams(
            collective_id=cid, has_side_effects=True, vmem_limit_bytes=62 * 1024 * 1024
        ),
    )(*arrays)


def finish(gains, attn_piece, out_piece, cid):
    F, C = lax.axis_size("fsdp"), lax.axis_size("ctx")
    dma = pltpu.SemaphoreType.DMA

    def kernel(g, a, w, g_out, a_out, w_out, gbox, gsum, cbox, gs, gr, cs, cr, as_, ar, ws, wr):
        f, c = lax.axis_index("fsdp"), lax.axis_index("ctx")
        goal = c * F + f
        gf, gc = goal // C, goal % C
        here = f * C + c
        sc, sf = here // F, here % F
        away = goal != here
        barrier = pltpu.get_barrier_semaphore()
        fpeer = [lax.rem(f + k, F) for k in range(F)]
        cpeer = [lax.rem(c + k, C) for k in range(C)]
        for k in range(1, F):
            pl.semaphore_signal(barrier, inc=1, device_id=(fpeer[k], c), device_id_type=MESH)
        for k in range(1, C):
            pl.semaphore_signal(barrier, inc=1, device_id=(f, cpeer[k]), device_id_type=MESH)

        @pl.when(away)
        def _():
            pl.semaphore_signal(barrier, inc=1, device_id=(sf, sc), device_id_type=MESH)

        pl.semaphore_wait(barrier, F + C - 2 + jnp.where(away, 1, 0))

        def gcopy(k):
            return remote(g.at[fpeer[k]], gbox.at[k - 1], gs.at[k], gr.at[k], (fpeer[k], c))

        def acopy(k):
            return remote(a.at[cpeer[k]], a_out.at[c], as_.at[k], ar.at[k], (f, cpeer[k]))

        def arecv(k):
            slot = a_out.at[lax.rem(c + C - k, C)]
            return remote(slot, slot, as_.at[k], ar.at[k], (f, cpeer[k]))

        def wcopy():
            return remote(w, w_out, ws.at[0], wr.at[0], (gf, gc))

        def ccopy(k):
            return remote(gsum, cbox.at[k - 1], cs.at[k], cr.at[k], (f, cpeer[k]))

        for k in range(1, F):
            gcopy(k).start()
        for k in range(1, C):
            acopy(k).start()

        @pl.when(away)
        def _():
            wcopy().start()

        @pl.when(jnp.logical_not(away))
        def _():
            w_out[...] = w[...]

        a_out[c] = a[c]
        total = g[f]
        for k in range(1, F):
            gcopy(k).wait_recv()
            total = total + gbox[k - 1]
        gsum[...] = total
        for k in range(1, C):
            ccopy(k).start()
        for k in range(1, C):
            ccopy(k).wait_recv()
            total = total + cbox[k - 1]
        g_out[...] = total
        for k in range(1, C):
            arecv(k).wait_recv()
        for k in range(1, F):
            gcopy(k).wait_send()
        for k in range(1, C):
            acopy(k).wait_send()
            ccopy(k).wait_send()

        @pl.when(away)
        def _():
            wcopy().wait()

    vm = pl.BlockSpec(memory_space=pltpu.VMEM)
    return pl.pallas_call(
        kernel,
        out_shape=[
            jax.ShapeDtypeStruct(gains.shape[1:], F32),
            jax.ShapeDtypeStruct(attn_piece.shape, attn_piece.dtype),
            jax.ShapeDtypeStruct(out_piece.shape, out_piece.dtype),
        ],
        in_specs=[vm] * 3,
        out_specs=[vm] * 3,
        scratch_shapes=[
            pltpu.VMEM((F - 1,) + gains.shape[1:], F32),
            pltpu.VMEM(gains.shape[1:], F32),
            pltpu.VMEM((C - 1,) + gains.shape[1:], F32),
        ]
        + [dma((F,)), dma((F,)), dma((C,)), dma((C,)), dma((C,)), dma((C,)), dma((1,)), dma((1,))],
        compiler_params=pltpu.CompilerParams(collective_id=cid, has_side_effects=True),
    )(gains, attn_piece, out_piece)


def on_device(
    block_input,
    attn_gain,
    query_proj,
    key_proj,
    value_proj,
    qk_gain,
    out_proj,
    ffn_gain,
    gate_proj,
    up_proj,
    down_proj,
    seg_lengths,
    out_cotangent,
):
    T, W = block_input.shape
    C = lax.axis_size("ctx")
    F = lax.axis_size("fsdp")
    L, D = factor("fsdp")
    CL, CD = factor("ctx")
    G = T * C
    hl, kl, share = H // C, KVH // C, H // KVH
    qw, kw = hl * HEAD, kl * HEAD
    rows = query_proj.shape[0]
    scale_att = HEAD ** (-0.5)
    c = lax.axis_index("ctx")

    w_own = jnp.concatenate(
        [
            lax.dynamic_slice_in_dim(query_proj, c * qw, qw, axis=1),
            lax.dynamic_slice_in_dim(key_proj, c * kw, kw, axis=1),
            lax.dynamic_slice_in_dim(value_proj, c * kw, kw, axis=1),
        ],
        axis=1,
    )
    gain_w, pair_w = attn_gain.shape[0], qk_gain.shape[0]
    g_own = jnp.zeros((16, 128), BF)
    g_own = g_own.at[0, :gain_w].set(attn_gain).at[1, :gain_w].set(ffn_gain)
    g_own = g_own.at[2, :pair_w].set(qk_gain)
    x_all, w_all, g_all, wo = communicate(
        [
            Gather("ctx", (T, W), BF, "line"),
            Gather("fsdp", w_own.shape, BF, "both"),
            Gather("fsdp", (16, 128), BF, "line"),
            Spread(out_proj.shape, BF, pieces(out_proj.shape[0], 4)),
        ],
        [block_input, w_own, g_own, out_proj],
        1,
    )
    x_all = x_all.reshape(G, W)
    w_all = w_all.reshape(W, qw + 2 * kw)
    wo = wo.reshape(qw, W)
    g_all = g_all.reshape(F, 16, 128)
    gain_attn = g_all[:, 0, :gain_w].reshape(W).astype(F32)
    gain_ffn = g_all[:, 1, :gain_w].reshape(W).astype(F32)
    gain_pair = g_all[:, 2, :pair_w].reshape(2 * HEAD).astype(F32)
    gain_query, gain_key = gain_pair[:HEAD], gain_pair[HEAD:]

    segment, positions = segment_positions(seg_lengths[0], G)
    cos_tab, sine_tab = rope_tables(positions, HEAD)
    xa = x_all.astype(F32)
    normed = (xa * rms_scale(xa) * gain_attn).astype(BF)
    qkv = dot_nn(normed, w_all)
    queries = qkv[:, :qw].reshape(G, hl, HEAD)
    keys_raw = qkv[:, qw : qw + kw].reshape(G, kl, HEAD)
    v_kv = qkv[:, qw + kw :].astype(BF).reshape(G, kl, HEAD)
    inv_query = rms_scale(queries)
    q_local = rotate(queries * inv_query * gain_query, cos_tab, sine_tab).astype(BF)
    inv_key = rms_scale(keys_raw)
    k_kv = rotate(keys_raw * inv_key * gain_key, cos_tab, sine_tab).astype(BF)
    k_local = jnp.repeat(k_kv, share, axis=1)
    v_local = jnp.repeat(v_kv, share, axis=1)
    token = jnp.arange(G, dtype=jnp.int32)
    allowed = (segment[:, None] == segment[None, :]) & (token[None, :] <= token[:, None])
    scores = (
        jnp.einsum("qhd,khd->hqk", q_local, k_local, preferred_element_type=F32) * scale_att
    )
    scores = jnp.where(allowed[None], scores, masked_score)
    top = jnp.max(scores, axis=2, keepdims=True)
    log_total = top + jnp.log(jnp.sum(jnp.exp(scores - top), axis=2, keepdims=True))
    prob_full = jnp.exp(scores - log_total)
    prob_bf = prob_full.astype(BF)
    o_local = jnp.einsum("hqk,khd->qhd", prob_bf, v_local, preferred_element_type=F32).astype(BF)
    o_flat = o_local.reshape(G, qw)
    part = dot_nn(o_flat, wo).astype(BF).reshape(CL, CD, T, W)
    attn_sum, dy_all = communicate(
        [Reduce("ctx", (T, W), BF, 4), Gather("fsdp", (T, W), BF, "both")],
        [part, out_cotangent],
        2,
    )
    dy_all = dy_all.reshape(F * T, W)

    x_float = block_input.astype(F32)
    inv_one = rms_scale(x_float)
    mixed_res = x_float + attn_sum
    inv_two = rms_scale(mixed_res)
    ffn_in = (mixed_res * inv_two * gain_ffn).astype(BF)
    (ffn_all,) = communicate([Gather("fsdp", (T, W), BF, "both")], [ffn_in], 3)
    ffn_all = ffn_all.reshape(F * T, W)
    gate_pre = dot_nt(ffn_all, gate_proj)
    up_pre = dot_nt(ffn_all, up_proj)
    gate_sig = jax.nn.sigmoid(gate_pre)
    active = gate_pre * gate_sig
    hidden = (active * up_pre).astype(BF)
    d_hidden = dot_nt(dy_all, down_proj)
    d_gate = (d_hidden * up_pre * gate_sig * (1.0 + gate_pre * (1.0 - gate_sig))).astype(BF)
    d_up = (d_hidden * active).astype(BF)
    ffc = gate_proj.shape[0] // C
    grads = [
        dot_tn(a, b).astype(BF).reshape(CL, CD, ffc, W)
        for a, b in ((d_gate, ffn_all), (d_up, ffn_all), (hidden, dy_all))
    ]
    down_part = dot_nn(hidden, down_proj).astype(BF).reshape(L, D, T, W)
    back_part = (
        (dot_nn(d_gate, gate_proj) + dot_nn(d_up, up_proj)).astype(BF).reshape(L, D, T, W)
    )
    gate_grad, up_grad, down_grad, d_ffn_in, ffn_out = communicate(
        [
            Reduce("ctx", (ffc, W), BF, 3, 0, 0),
            Reduce("ctx", (ffc, W), BF, 3, 0, 3),
            Reduce("ctx", (ffc, W), BF, 3, 0, 6),
            Reduce("fsdp", (T, W), BF, 8, 1, 0),
            Reduce("fsdp", (T, W), BF, 8, 2, 7),
        ],
        grads + [back_part, down_part],
        4,
    )
    block_output = (mixed_res + ffn_out).astype(BF)
    grad_gain_ffn = jnp.sum(d_ffn_in * mixed_res * inv_two, axis=0)
    d_mixed = out_cotangent.astype(F32) + norm_back(mixed_res, inv_two, gain_ffn, d_ffn_in)
    (dm_all,) = communicate([Gather("ctx", (T, W), BF, "line")], [d_mixed.astype(BF)], 5)
    dm_all = dm_all.reshape(G, W)
    d_local = dot_nt(dm_all, wo).astype(BF).reshape(G, hl, HEAD)
    row_delta = jnp.sum(d_local.astype(F32) * o_local.astype(F32), axis=2).T[:, :, None]
    d_prob = jnp.einsum("qhd,khd->hqk", d_local, v_local, preferred_element_type=F32)
    d_score = (prob_full * (d_prob - row_delta) * scale_att).astype(BF)
    dq_rot = jnp.einsum("hqk,khd->qhd", d_score, k_local, preferred_element_type=F32).astype(BF)
    dk_sum = jnp.einsum("hqk,qhd->khd", d_score, q_local, preferred_element_type=F32)
    dv_sum = jnp.einsum("hqk,qhd->khd", prob_bf, d_local, preferred_element_type=F32)
    dk_rot = jnp.sum(dk_sum.reshape(G, kl, share, HEAD), axis=2).astype(BF)
    d_values = jnp.sum(dv_sum.reshape(G, kl, share, HEAD), axis=2).astype(BF)
    d_q_norm = unrotate(dq_rot.astype(F32), cos_tab, sine_tab)
    d_k_norm = unrotate(dk_rot.astype(F32), cos_tab, sine_tab)
    grad_gain_q = jnp.sum(d_q_norm * queries * inv_query, axis=(0, 1))
    grad_gain_k = jnp.sum(d_k_norm * keys_raw * inv_key, axis=(0, 1))
    d_queries = norm_back(queries, inv_query, gain_query, d_q_norm).astype(BF).reshape(G, qw)
    d_keys = norm_back(keys_raw, inv_key, gain_key, d_k_norm).astype(BF).reshape(G, kw)
    d_qkv = jnp.concatenate([d_queries, d_keys, d_values.reshape(G, kw)], axis=1)
    dn_part = dot_nt(d_qkv, w_all).astype(BF).reshape(CL, CD, T, W)
    qkv_part = dot_tn(normed, d_qkv).astype(BF).reshape(L, D, rows, qw + 2 * kw)
    wo_part = dot_tn(o_flat, dm_all).astype(BF).reshape(L, D, qw // F, W)
    d_normed, qkv_sum, wo_sum = communicate(
        [
            Reduce("ctx", (T, W), BF, 4),
            Reduce("fsdp", qkv_part.shape[2:], BF, 4, 0, 0),
            Reduce("fsdp", wo_part.shape[2:], BF, 2, 1, 4),
        ],
        [dn_part, qkv_part, wo_part],
        6,
    )
    grad_gain_attn = jnp.sum(d_normed * x_float * inv_one, axis=0)
    input_grad = d_mixed + norm_back(x_float, inv_one, gain_attn, d_normed)
    pair = jnp.concatenate([grad_gain_q, grad_gain_k]).reshape(F, 1, pair_w)
    gains = jnp.zeros((F, 8, 128), F32)
    gains = gains.at[:, 0:1, :gain_w].set(grad_gain_attn.reshape(F, 1, gain_w))
    gains = gains.at[:, 1:2, :gain_w].set(grad_gain_ffn.reshape(F, 1, gain_w))
    gains = gains.at[:, 2:3, :pair_w].set(pair)
    g_sum, a_out, out_proj_grad = finish(
        gains,
        qkv_sum.astype(BF).reshape(C, rows // C, qw + 2 * kw),
        wo_sum.astype(BF),
        7,
    )
    a_out = a_out.astype(F32)
    own_rows = rows // C
    query_grad = a_out[:, :, :qw].transpose(1, 0, 2).reshape(own_rows, C * qw)
    key_grad = a_out[:, :, qw : qw + kw].transpose(1, 0, 2).reshape(own_rows, C * kw)
    value_grad = a_out[:, :, qw + kw :].transpose(1, 0, 2).reshape(own_rows, C * kw)
    return (
        block_output,
        input_grad,
        g_sum[0, :gain_w],
        query_grad,
        key_grad,
        value_grad,
        g_sum[2, :pair_w],
        out_proj_grad.astype(F32),
        g_sum[1, :gain_w],
        gate_grad,
        up_grad,
        down_grad,
    )


def solution(mesh):
    return jax.shard_map(
        on_device,
        mesh=mesh,
        in_specs=(
            P(("fsdp", "ctx"), None),
            P("fsdp"),
            P("fsdp", None),
            P("fsdp", None),
            P("fsdp", None),
            P("fsdp"),
            P("fsdp", None),
            P("fsdp"),
            P("fsdp", None),
            P("fsdp", None),
            P("fsdp", None),
            P("fsdp", None),
            P(("fsdp", "ctx"), None),
        ),
        out_specs=(
            P(("fsdp", "ctx"), None),
            P(("fsdp", "ctx"), None),
            P("fsdp"),
            P(("fsdp", "ctx"), None),
            P(("fsdp", "ctx"), None),
            P(("fsdp", "ctx"), None),
            P("fsdp"),
            P(("fsdp", "ctx"), None),
            P("fsdp"),
            P(("fsdp", "ctx"), None),
            P(("fsdp", "ctx"), None),
            P(("fsdp", "ctx"), None),
        ),
        check_vma=False,
    )
```

```python
import jax
import jax.numpy as jnp
from jax import lax
from jax.experimental import pallas as pl
from jax.experimental.pallas import tpu as pltpu
from jax.sharding import PartitionSpec as P

H = 16
KVH = 8
HEAD = 64


epsilon = 1e-05
rope_base = 1000000.0
masked_score = -1e30


def rms_scale(values):
    return lax.rsqrt(jnp.mean(values * values, axis=-1, keepdims=True) + epsilon)


def norm_back(values, inv_rms, gain_vec, upstream):
    scaled_up = upstream * gain_vec
    return inv_rms * scaled_up - values * (inv_rms * inv_rms * inv_rms) * jnp.mean(
        scaled_up * values, axis=-1, keepdims=True
    )


def segment_positions(lengths, token_count):
    seg_ends = jnp.cumsum(lengths)
    seg_starts = seg_ends - lengths
    token_index = jnp.arange(token_count, dtype=jnp.int32)
    segment = jnp.sum((token_index[:, None] >= seg_ends[None, :]).astype(jnp.int32), axis=1)
    seg_begin = jnp.max(
        jnp.where(token_index[:, None] >= seg_starts[None, :], seg_starts[None, :], 0), axis=1
    )
    return (segment, token_index - seg_begin)


def rope_tables(positions, head_width):
    half_width = head_width // 2
    frequency = rope_base ** (-(jnp.arange(half_width, dtype=jnp.float32) * 2.0 / head_width))
    angle_all = positions.astype(jnp.float32)[:, None] * frequency[None, :]
    return (jnp.cos(angle_all), jnp.sin(angle_all))


def rotate(values, cos_tab, sine_tab):
    half_width = values.shape[-1] // 2
    front_half = values[..., :half_width]
    back_half = values[..., half_width:]
    cos_b = cos_tab[:, None, :]
    sin_b = sine_tab[:, None, :]
    return jnp.concatenate(
        [front_half * cos_b - back_half * sin_b, back_half * cos_b + front_half * sin_b], axis=-1
    )


def unrotate(upstream, cos_tab, sine_tab):
    half_width = upstream.shape[-1] // 2
    front_half = upstream[..., :half_width]
    back_half = upstream[..., half_width:]
    cos_b = cos_tab[:, None, :]
    sin_b = sine_tab[:, None, :]
    return jnp.concatenate(
        [front_half * cos_b + back_half * sin_b, back_half * cos_b - front_half * sin_b], axis=-1
    )


def dot_nn(left_mat, right_mat):
    return jnp.dot(left_mat, right_mat, preferred_element_type=jnp.float32)


def dot_nt(left_mat, right_mat):
    return lax.dot_general(
        left_mat, right_mat, (((1,), (1,)), ((), ())), preferred_element_type=jnp.float32
    )


def dot_tn(left_mat, right_mat):
    return lax.dot_general(
        left_mat, right_mat, (((0,), (0,)), ((), ())), preferred_element_type=jnp.float32
    )


MESH = pl.DeviceIdType.MESH
BF = jnp.bfloat16
F32 = jnp.float32


def factor(name):
    count = lax.axis_size(name)
    if name == "ctx":
        direct = 2
    else:
        direct = 1
        while direct * direct * 4 <= count:
            direct *= 2
    return count // direct, direct


class Place:
    def __init__(self, name):
        self.name = name
        self.L, self.D = factor(name)
        index = lax.axis_index(name)
        self.l = index // self.D
        self.d = index % self.D

    def dev(self, l, d):
        return {self.name: l * self.D + d}

    def off(self, dd):
        return lax.rem(self.d + dd, self.D)


def remote(src, dst, ssem, rsem, dev):
    return pltpu.make_async_remote_copy(
        src_ref=src, dst_ref=dst, send_sem=ssem, recv_sem=rsem, device_id=dev, device_id_type=MESH
    )


def add_rows(dst, parts, lead):
    rows = dst.shape[-2]
    step = 16 if rows % 16 == 0 else rows

    def one(pick):
        def body(i, carry):
            at = pl.ds(pl.multiple_of(i * step, step), step) if step != rows else slice(None)
            if dst.dtype == BF and len(parts) == 2:
                pick(dst)[at, :] = pick(parts[0])[at, :] + pick(parts[1])[at, :]
                return carry
            total = pick(parts[0])[at, :].astype(F32)
            for part in parts[1:]:
                total = total + pick(part)[at, :].astype(F32)
            pick(dst)[at, :] = total.astype(dst.dtype)
            return carry

        if step == rows:
            body(0, 0)
        else:
            lax.fori_loop(0, rows // step, body, 0)

    if lead is None:
        one(lambda ref: ref)
    else:
        for j in range(lead):
            one(lambda ref, j=j: ref.at[j])


def line_neighbors(p, act):
    @pl.when(p.l > 0)
    def _():
        act(-1)

    @pl.when(p.l < p.L - 1)
    def _():
        act(1)


def pieces(rows, most):
    for count in range(most, 1, -1):
        if rows % (16 * count) == 0:
            return count
    return 1


def cut(first, rows, size):
    res = []
    while rows > 0:
        take = min(size, rows)
        res.append((first, take, "line"))
        first, rows = first + take, rows - take
    return res


class Gather:
    def __init__(self, name, shape, dtype, split):
        self.name, self.shape, self.dtype = name, shape, dtype
        self.L, self.D = factor(name)
        rows = shape[0]
        self.parts = []
        if split == "both":
            units = rows // 16
            lead = max(1, units // 8)
            self.parts = cut(0, rows - lead * 16, 32) + [(rows - lead * 16, lead * 16, "dir")]
        elif pieces(rows, 4) > 1:
            count = pieces(rows, 4)
            size = rows // count
            self.parts = [(i * size, size, split) for i in range(count)]
        else:
            self.parts = [(0, rows, split)]
        self.outs = [jax.ShapeDtypeStruct((self.L, self.D) + shape, dtype)]
        self.scratch = []
        dma = pltpu.SemaphoreType.DMA
        L, D = self.L, self.D
        for _, _, kind in self.parts:
            if kind == "line":
                self.scratch += [dma((2, L)), dma((L,)), dma((D, L)), dma((D, L))]
            else:
                self.scratch += [dma((D,)), dma((D,)), dma((D, 2, L)), dma((D, L))]

    def gens(self, p, ins, outs, scr):
        src, out = ins[0], outs[0]
        res = []
        for i, (r0, r, kind) in enumerate(self.parts):
            f = self.line_first if kind == "line" else self.dir_first
            res.append((0, f(p, src, out, r0, r, scr[4 * i : 4 * i + 4], i == 0)))
        return res

    def line_first(self, p, src, out, r0, r, sems, keep):
        ls, lr, ds, dr = sems
        L, D, l, d = p.L, p.D, p.l, p.d
        own = src.at[pl.ds(r0, r), :]

        def V(q, dd):
            return out.at[q, dd, pl.ds(r0, r), :]

        def line(q, dirn, view):
            return remote(view, V(q, d), ls.at[(dirn + 1) // 2, q], lr.at[q], p.dev(l + dirn, d))

        def direct(q, view, k):
            return remote(view, V(q, d), ds.at[k - 1, q], dr.at[k - 1, q], p.dev(l, p.off(k)))

        line_neighbors(p, lambda dirn: line(l, dirn, own).start())
        for k in range(1, D):
            direct(l, own, k).start()
        if keep:
            out[l, d] = src[...]
        yield
        for k in range(1, L):
            for sgn in (-1, 1):
                q = l + sgn * k

                @pl.when((q >= 0) & (q < L))
                def _(q=q, sgn=sgn):
                    line(q, -sgn, V(q, d)).wait_recv()
                    for m in range(1, D):
                        direct(q, V(q, d), m).start()

                    @pl.when((l - sgn >= 0) & (l - sgn < L))
                    def _():
                        line(q, -sgn, V(q, d)).start()

            yield
        for q in range(L):
            for k in range(1, D):
                w = V(q, p.off(D - k))
                remote(w, w, ds.at[k - 1, q], dr.at[k - 1, q], p.dev(l, p.off(k))).wait_recv()
        yield "drain"
        for q in range(L):
            for k in range(1, D):
                direct(q, V(q, d), k).wait_send()
        for k in range(0, L):
            for sgn in (-1, 1):
                if k == 0:
                    q = l

                    @pl.when((l - sgn >= 0) & (l - sgn < L))
                    def _(sgn=sgn):
                        line(l, -sgn, own).wait_send()
                else:
                    q = l + sgn * k

                    @pl.when((q >= 0) & (q < L) & (l - sgn >= 0) & (l - sgn < L))
                    def _(q=q, sgn=sgn):
                        line(q, -sgn, V(q, d)).wait_send()

    def dir_first(self, p, src, out, r0, r, sems, keep):
        ds, dr, ls, lr = sems
        L, D, l, d = p.L, p.D, p.l, p.d
        own = src.at[pl.ds(r0, r), :]

        def V(q, dd):
            return out.at[q, dd, pl.ds(r0, r), :]

        def line(j, q, dirn, view):
            return remote(
                view,
                V(q, p.off(D - j)),
                ls.at[j, (dirn + 1) // 2, q],
                lr.at[j, q],
                p.dev(l + dirn, d),
            )

        def direct(k):
            return remote(own, V(l, d), ds.at[k - 1], dr.at[k - 1], p.dev(l, p.off(k)))

        for k in range(1, D):
            direct(k).start()
        line_neighbors(p, lambda dirn: line(0, l, dirn, own).start())
        if keep:
            out[l, d] = src[...]
        yield
        for j in range(1, D):
            w = V(l, p.off(D - j))
            remote(w, w, ds.at[j - 1], dr.at[j - 1], p.dev(l, p.off(j))).wait_recv()
            line_neighbors(p, lambda dirn: line(j, l, dirn, w).start())
        yield
        for k in range(1, L):
            for j in range(D):
                for sgn in (-1, 1):
                    q = l + sgn * k

                    @pl.when((q >= 0) & (q < L))
                    def _(q=q, sgn=sgn, j=j):
                        w = V(q, p.off(D - j))
                        line(j, q, -sgn, w).wait_recv()

                        @pl.when((l - sgn >= 0) & (l - sgn < L))
                        def _():
                            line(j, q, -sgn, w).start()

            yield "drain" if k == L - 1 else None
        for k in range(1, D):
            direct(k).wait_send()
        for k in range(0, L):
            for j in range(D):
                for sgn in (-1, 1):
                    q = l + sgn * k if k else l

                    @pl.when((q >= 0) & (q < L) & (l - sgn >= 0) & (l - sgn < L))
                    def _(q=q, sgn=sgn, j=j):
                        line(j, q, -sgn, own if (k == 0 and j == 0) else V(q, p.off(D - j))).wait_send()


class Spread:
    def __init__(self, shape, dtype, chunks):
        self.shape, self.dtype, self.chunks = shape, dtype, chunks
        self.L, self.D = factor("fsdp")
        if lax.axis_size("ctx") != self.L:
            raise ValueError("unsupported mesh")
        self.name = "fsdp"
        self.outs = [jax.ShapeDtypeStruct((self.D,) + shape, dtype)]
        dma = pltpu.SemaphoreType.DMA
        self.scratch = [dma((chunks, 2)), dma((chunks,)), dma((chunks, self.D)), dma((chunks, self.D))]

    def gens(self, p, ins, outs, scr):
        rows = self.shape[0] // self.chunks
        return [(i, self.one(p, ins[0], outs[0], i, rows, scr)) for i in range(self.chunks)]

    def one(self, p, src, out, i, rows, scr):
        ls, lr, ds, dr = scr
        l, d, D = p.l, p.d, p.D
        c = lax.axis_index("ctx")
        own = src.at[pl.ds(i * rows, rows), :]
        at_home = l == c

        def V(dd):
            return out.at[dd, pl.ds(i * rows, rows), :]

        def line(dirn, view):
            return remote(view, V(d), ls.at[i, (dirn + 1) // 2], lr.at[i], p.dev(l + dirn, d))

        def direct(k, view):
            return remote(view, V(d), ds.at[i, k - 1], dr.at[i, k - 1], p.dev(l, p.off(k)))

        @pl.when(at_home)
        def _():
            line_neighbors(p, lambda dirn: line(dirn, own).start())
            for k in range(1, D):
                direct(k, own).start()
            if i == 0:
                out[d] = src[...]

        yield

        @pl.when(l > c)
        def _():
            line(1, V(d)).wait_recv()

            @pl.when(l < p.L - 1)
            def _():
                line(1, V(d)).start()

            for k in range(1, D):
                direct(k, V(d)).start()

        @pl.when(l < c)
        def _():
            line(-1, V(d)).wait_recv()

            @pl.when(l > 0)
            def _():
                line(-1, V(d)).start()

            for k in range(1, D):
                direct(k, V(d)).start()

        yield
        for k in range(1, D):
            w = V(p.off(D - k))
            remote(w, w, ds.at[i, k - 1], dr.at[i, k - 1], p.dev(l, p.off(k))).wait_recv()
        yield "drain"
        for k in range(1, D):
            direct(k, V(d)).wait_send()

        @pl.when((l <= c) & (l > 0))
        def _():
            line(-1, V(d)).wait_send()

        @pl.when((l >= c) & (l < p.L - 1))
        def _():
            line(1, V(d)).wait_send()


class Reduce:
    def __init__(self, name, shape, dtype, most=1, lines=0, first=0, result=F32):
        self.name, self.shape, self.dtype, self.first = name, shape, dtype, first
        self.L, self.D = factor(name)
        L, D = self.L, self.D
        self.outs = [jax.ShapeDtypeStruct(shape, result)]
        dma = pltpu.SemaphoreType.DMA
        self.count = pieces(shape[0], most if L * D <= 8 else min(most, 4))
        unit = (shape[0] // self.count,) + shape[1:]
        self.scratch = []
        self.kinds = ["dir"] * (self.count - lines) + ["line"] * min(lines, self.count)
        for kind in self.kinds:
            if kind == "line":
                self.scratch += [
                    pltpu.VMEM((L, D) + unit, dtype),
                    pltpu.VMEM((L, D) + unit, dtype),
                    pltpu.VMEM((D,) + unit, dtype),
                    pltpu.VMEM((max(D - 1, 1),) + unit, dtype),
                    dma((2, L)),
                    dma((2, L)),
                    dma((D,)),
                    dma((D,)),
                ]
            else:
                self.scratch += [
                    pltpu.VMEM((L,) + unit, dtype),
                    pltpu.VMEM((L,) + unit, dtype),
                    pltpu.VMEM((L,) + unit, dtype),
                    pltpu.VMEM((max(D - 1, 1), L) + unit, dtype),
                    dma((2, L)),
                    dma((2, L)),
                    dma((D, L)),
                    dma((D, L)),
                ]

    def gens(self, p, ins, outs, scr):
        size = self.shape[0] // self.count
        res = []
        for i, kind in enumerate(self.kinds):
            at = pl.ds(i * size, size)
            f = self.line_first if kind == "line" else self.dir_first
            start = 0 if kind == "line" else self.first + i
            res.append((start, f(p, ins[0], outs[0].at[at, :], at, scr[8 * i : 8 * i + 8])))
        return res

    def line_sum(self, p, own, from_left, from_right, ls, lr, lead, prep):
        L, l = p.L, p.l

        def right(q, view):
            return remote(view, from_left.at[q], ls.at[1, q], lr.at[1, q], p.dev(l + 1, p.d))

        def left(q, view):
            return remote(view, from_right.at[q], ls.at[0, q], lr.at[0, q], p.dev(l - 1, p.d))

        for t in range(L):
            qr, ql = L - 1 - t, t
            prep(qr)
            if qr > 0:

                @pl.when(l == 0)
                def _():
                    right(qr, own(qr)).start()

            prep(ql)
            if ql < L - 1:

                @pl.when(l == L - 1)
                def _():
                    left(ql, own(ql)).start()

        yield "late" if L <= 2 else None
        for k in range(1, L - 1):

            @pl.when(l == k)
            def _():
                for q in range(L - 1, k, -1):
                    right(q, from_left.at[q]).wait_recv()
                    add_rows(from_left.at[q], [from_left.at[q], own(q)], lead)
                    right(q, from_left.at[q]).start()

            @pl.when(l == L - 1 - k)
            def _():
                for q in range(L - 1 - k):
                    left(q, from_right.at[q]).wait_recv()
                    add_rows(from_right.at[q], [from_right.at[q], own(q)], lead)
                    left(q, from_right.at[q]).start()

            yield

    def line_total(self, p, own, from_left, from_right, ls, lr, dst, lead):
        l, L = p.l, p.L

        def arrive(way):
            v = (from_left if way == 1 else from_right).at[l]
            remote(v, v, ls.at[way, l], lr.at[way, l], p.dev(l + 1 - 2 * way, p.d)).wait_recv()

        @pl.when(l == 0)
        def _():
            arrive(0)
            add_rows(dst, [own(l), from_right.at[l]], lead)

        @pl.when(l == L - 1)
        def _():
            arrive(1)
            add_rows(dst, [own(l), from_left.at[l]], lead)

        if L > 2:

            @pl.when((l > 0) & (l < L - 1))
            def _():
                arrive(0)
                arrive(1)
                add_rows(dst, [own(l), from_left.at[l], from_right.at[l]], lead)

    def line_drain(self, p, from_left, from_right, ls, lr):
        L, l = p.L, p.l
        for q in range(L):
            if q > 0:

                @pl.when(l < q)
                def _():
                    v = from_left.at[q]
                    remote(v, v, ls.at[1, q], lr.at[1, q], p.dev(l + 1, p.d)).wait_send()

            if q < L - 1:

                @pl.when(l > q)
                def _():
                    v = from_right.at[q]
                    remote(v, v, ls.at[0, q], lr.at[0, q], p.dev(l - 1, p.d)).wait_send()

    def line_first(self, p, src, out, at, scr):
        from_left, from_right, acc, box, ls, lr, ds, dr = scr
        D, l, d = p.D, p.l, p.d

        def own(q):
            return src.at[q, :, at, :]

        yield from self.line_sum(p, own, from_left, from_right, ls, lr, D, lambda q: None)
        self.line_total(p, own, from_left, from_right, ls, lr, acc, D)

        def direct(k):
            return remote(
                acc.at[p.off(k)], box.at[k - 1], ds.at[k - 1], dr.at[k - 1], p.dev(l, p.off(k))
            )

        for k in range(1, D):
            direct(k).start()
        yield "late" if self.L > 2 else None
        for k in range(1, D):
            direct(k).wait_recv()
        add_rows(out, [acc.at[d]] + [box.at[k - 1] for k in range(1, D)], None)
        yield "drain"
        for k in range(1, D):
            direct(k).wait_send()
        self.line_drain(p, from_left, from_right, ls, lr)

    def dir_first(self, p, src, out, at, scr):
        from_left, from_right, acc, box, ls, lr, ds, dr = scr
        L, D, l, d = p.L, p.D, p.l, p.d

        def direct(k, q):
            return remote(
                src.at[q, p.off(k), at, :],
                box.at[k - 1, q],
                ds.at[k - 1, q],
                dr.at[k - 1, q],
                p.dev(l, p.off(k)),
            )

        order = []
        for t in range(L):
            for q in (L - 1 - t, t):
                if q not in order:
                    order.append(q)
        for q in order:
            for k in range(1, D):
                direct(k, q).start()
        yield
        ready = set()

        def prep(q):
            if q in ready:
                return
            ready.add(q)
            for k in range(1, D):
                direct(k, q).wait_recv()
            add_rows(
                acc.at[q], [src.at[q, d, at, :]] + [box.at[k - 1, q] for k in range(1, D)], None
            )

        def own(q):
            return acc.at[q]

        yield from self.line_sum(p, own, from_left, from_right, ls, lr, None, prep)
        self.line_total(p, own, from_left, from_right, ls, lr, out, None)
        yield "drain"
        for q in range(L):
            for k in range(1, D):
                direct(k, q).wait_send()
        self.line_drain(p, from_left, from_right, ls, lr)


def greet(places):
    barrier = pltpu.get_barrier_semaphore()
    count = 0
    for p in places:
        for k in range(1, p.D):
            pl.semaphore_signal(
                barrier, inc=1, device_id=p.dev(p.l, p.off(k)), device_id_type=MESH
            )
        count = count + (p.D - 1)
        line_neighbors(
            p,
            lambda dirn: pl.semaphore_signal(
                barrier, inc=1, device_id=p.dev(p.l + dirn, p.d), device_id_type=MESH
            ),
        )
        count = count + jnp.where(p.l > 0, 1, 0) + jnp.where(p.l < p.L - 1, 1, 0)
    pl.semaphore_wait(barrier, count)


def run_all(live):
    live = sorted(live, key=lambda pair: pair[0])
    late, drains, slot = [], [], 0
    while live:
        for start, g in live:
            if start == slot:
                next(g)
        rest = []
        for start, g in live:
            if start >= slot:
                rest.append((start, g))
                continue
            mark = next(g)
            if mark == "drain":
                drains.append(g)
            elif mark == "late":
                late.append(g)
            else:
                rest.append((start, g))
        live, slot = rest, slot + 1
    for g in late + drains:
        for _ in g:
            pass


def communicate(ops, arrays, cid):
    axes = sorted({op.name for op in ops})
    outs = [shape for op in ops for shape in op.outs]
    scratch = [s for op in ops for s in op.scratch]

    def kernel(*refs):
        ins = refs[: len(arrays)]
        out_refs = refs[len(arrays) : len(arrays) + len(outs)]
        scr = refs[len(arrays) + len(outs) :]
        places = {name: Place(name) for name in axes}
        greet([places[name] for name in axes])
        live = []
        o = s = 0
        for i, op in enumerate(ops):
            live += op.gens(
                places[op.name],
                [ins[i]],
                out_refs[o : o + len(op.outs)],
                scr[s : s + len(op.scratch)],
            )
            o += len(op.outs)
            s += len(op.scratch)
        run_all(live)

    vm = pl.BlockSpec(memory_space=pltpu.VMEM)
    return pl.pallas_call(
        kernel,
        out_shape=outs,
        in_specs=[vm] * len(arrays),
        out_specs=[vm] * len(outs),
        scratch_shapes=scratch,
        compiler_params=pltpu.CompilerParams(
            collective_id=cid, has_side_effects=True, vmem_limit_bytes=62 * 1024 * 1024
        ),
    )(*arrays)


def finish(gains, attn_piece, out_piece, qw, kw, cid):
    F, C = lax.axis_size("fsdp"), lax.axis_size("ctx")
    dma = pltpu.SemaphoreType.DMA

    def kernel(
        g, a, w, g_out, q_out, k_out, v_out, o_out,
        gbox, gsum, cbox, a_out, w_out, gs, gr, cs, cr, as_, ar, ws, wr
    ):
        f, c = lax.axis_index("fsdp"), lax.axis_index("ctx")
        goal = c * F + f
        gf, gc = goal // C, goal % C
        here = f * C + c
        sc, sf = here // F, here % F
        away = goal != here
        barrier = pltpu.get_barrier_semaphore()
        fpeer = [lax.rem(f + k, F) for k in range(F)]
        cpeer = [lax.rem(c + k, C) for k in range(C)]
        for k in range(1, F):
            pl.semaphore_signal(barrier, inc=1, device_id=(fpeer[k], c), device_id_type=MESH)
        for k in range(1, C):
            pl.semaphore_signal(barrier, inc=1, device_id=(f, cpeer[k]), device_id_type=MESH)

        @pl.when(away)
        def _():
            pl.semaphore_signal(barrier, inc=1, device_id=(sf, sc), device_id_type=MESH)

        pl.semaphore_wait(barrier, F + C - 2 + jnp.where(away, 1, 0))

        def gcopy(k):
            return remote(g.at[fpeer[k]], gbox.at[k - 1], gs.at[k], gr.at[k], (fpeer[k], c))

        def acopy(k):
            return remote(a.at[cpeer[k]], a_out.at[c], as_.at[k], ar.at[k], (f, cpeer[k]))

        def arecv(k):
            slot = a_out.at[lax.rem(c + C - k, C)]
            return remote(slot, slot, as_.at[k], ar.at[k], (f, cpeer[k]))

        def wcopy():
            return remote(w, w_out, ws.at[0], wr.at[0], (gf, gc))

        def ccopy(k):
            return remote(gsum, cbox.at[k - 1], cs.at[k], cr.at[k], (f, cpeer[k]))

        for k in range(1, F):
            gcopy(k).start()
        for k in range(1, C):
            acopy(k).start()

        @pl.when(away)
        def _():
            wcopy().start()

        @pl.when(jnp.logical_not(away))
        def _():
            w_out[...] = w[...]

        a_out[c] = a[c]
        total = g[f]
        for k in range(1, F):
            gcopy(k).wait_recv()
            total = total + gbox[k - 1]
        gsum[...] = total
        for k in range(1, C):
            ccopy(k).start()
        for k in range(1, C):
            ccopy(k).wait_recv()
            total = total + cbox[k - 1]
        g_out[...] = total
        for k in range(1, C):
            arecv(k).wait_recv()
        for s in range(C):
            q_out[:, s * qw : (s + 1) * qw] = a_out[s, :, :qw].astype(F32)
            k_out[:, s * kw : (s + 1) * kw] = a_out[s, :, qw : qw + kw].astype(F32)
            v_out[:, s * kw : (s + 1) * kw] = a_out[s, :, qw + kw :].astype(F32)
        for k in range(1, F):
            gcopy(k).wait_send()
        for k in range(1, C):
            acopy(k).wait_send()
            ccopy(k).wait_send()

        @pl.when(away)
        def _():
            wcopy().wait()

        o_out[...] = w_out[...].astype(F32)

    rows = attn_piece.shape[1]
    vm = pl.BlockSpec(memory_space=pltpu.VMEM)
    return pl.pallas_call(
        kernel,
        out_shape=[
            jax.ShapeDtypeStruct(gains.shape[1:], F32),
            jax.ShapeDtypeStruct((rows, C * qw), F32),
            jax.ShapeDtypeStruct((rows, C * kw), F32),
            jax.ShapeDtypeStruct((rows, C * kw), F32),
            jax.ShapeDtypeStruct(out_piece.shape, F32),
        ],
        in_specs=[vm] * 3,
        out_specs=[vm] * 5,
        scratch_shapes=[
            pltpu.VMEM((F - 1,) + gains.shape[1:], F32),
            pltpu.VMEM(gains.shape[1:], F32),
            pltpu.VMEM((C - 1,) + gains.shape[1:], F32),
            pltpu.VMEM(attn_piece.shape, attn_piece.dtype),
            pltpu.VMEM(out_piece.shape, out_piece.dtype),
        ]
        + [dma((F,)), dma((F,)), dma((C,)), dma((C,)), dma((C,)), dma((C,)), dma((1,)), dma((1,))],
        compiler_params=pltpu.CompilerParams(collective_id=cid, has_side_effects=True),
    )(gains, attn_piece, out_piece)


def on_device(
    block_input,
    attn_gain,
    query_proj,
    key_proj,
    value_proj,
    qk_gain,
    out_proj,
    ffn_gain,
    gate_proj,
    up_proj,
    down_proj,
    seg_lengths,
    out_cotangent,
):
    T, W = block_input.shape
    C = lax.axis_size("ctx")
    F = lax.axis_size("fsdp")
    L, D = factor("fsdp")
    CL, CD = factor("ctx")
    G = T * C
    hl, kl, share = H // C, KVH // C, H // KVH
    qw, kw = hl * HEAD, kl * HEAD
    rows = query_proj.shape[0]
    scale_att = HEAD ** (-0.5)
    c = lax.axis_index("ctx")

    w_own = jnp.concatenate(
        [
            lax.dynamic_slice_in_dim(query_proj, c * qw, qw, axis=1),
            lax.dynamic_slice_in_dim(key_proj, c * kw, kw, axis=1),
            lax.dynamic_slice_in_dim(value_proj, c * kw, kw, axis=1),
        ],
        axis=1,
    )
    gain_w, pair_w = attn_gain.shape[0], qk_gain.shape[0]
    g_own = jnp.concatenate(
        [
            jnp.pad(vec[None, :], ((0, 0), (0, 128 - vec.shape[0])))
            for vec in (attn_gain, ffn_gain, qk_gain)
        ]
        + [jnp.zeros((13, 128), BF)],
        axis=0,
    )
    w_all, g_all, wo, x_all = communicate(
        [
            Gather("fsdp", w_own.shape, BF, "both"),
            Gather("fsdp", (16, 128), BF, "line"),
            Spread(out_proj.shape, BF, pieces(out_proj.shape[0], 4)),
            Gather("ctx", (T, W), BF, "line"),
        ],
        [w_own, g_own, out_proj, block_input],
        1,
    )
    x_all = x_all.reshape(G, W)
    w_all = w_all.reshape(W, qw + 2 * kw)
    wo = wo.reshape(qw, W)
    g_all = g_all.reshape(F, 16, 128)
    gain_attn = g_all[:, 0, :gain_w].reshape(W).astype(F32)
    gain_ffn = g_all[:, 1, :gain_w].reshape(W).astype(F32)
    gain_pair = g_all[:, 2, :pair_w].reshape(2 * HEAD).astype(F32)
    gain_query, gain_key = gain_pair[:HEAD], gain_pair[HEAD:]

    segment, positions = segment_positions(seg_lengths[0], G)
    cos_tab, sine_tab = rope_tables(positions, HEAD)
    xa = x_all.astype(F32)
    normed = (xa * rms_scale(xa) * gain_attn).astype(BF)
    qkv = dot_nn(normed, w_all)
    queries = qkv[:, :qw].reshape(G, hl, HEAD)
    keys_raw = qkv[:, qw : qw + kw].reshape(G, kl, HEAD)
    v_kv = qkv[:, qw + kw :].astype(BF).reshape(G, kl, HEAD)
    inv_query = rms_scale(queries)
    q_local = rotate(queries * inv_query * gain_query, cos_tab, sine_tab).astype(BF)
    inv_key = rms_scale(keys_raw)
    k_kv = rotate(keys_raw * inv_key * gain_key, cos_tab, sine_tab).astype(BF)
    k_local = jnp.repeat(k_kv, share, axis=1)
    v_local = jnp.repeat(v_kv, share, axis=1)
    token = jnp.arange(G, dtype=jnp.int32)
    allowed = (segment[:, None] == segment[None, :]) & (token[None, :] <= token[:, None])
    scores = (
        jnp.einsum("qhd,khd->hqk", q_local, k_local, preferred_element_type=F32) * scale_att
    )
    scores = jnp.where(allowed[None], scores, masked_score)
    top = jnp.max(scores, axis=2, keepdims=True)
    log_total = top + jnp.log(jnp.sum(jnp.exp(scores - top), axis=2, keepdims=True))
    prob_full = jnp.exp(scores - log_total)
    prob_bf = prob_full.astype(BF)
    o_local = jnp.einsum("hqk,khd->qhd", prob_bf, v_local, preferred_element_type=F32).astype(BF)
    o_flat = o_local.reshape(G, qw)
    part = dot_nn(o_flat, wo).astype(BF).reshape(CL, CD, T, W)
    attn_sum, dy_all = communicate(
        [Reduce("ctx", (T, W), BF, 2), Gather("fsdp", (T, W), BF, "both")],
        [part, out_cotangent],
        2,
    )
    dy_all = dy_all.reshape(F * T, W)

    x_float = block_input.astype(F32)
    inv_one = rms_scale(x_float)
    mixed_res = x_float + attn_sum
    inv_two = rms_scale(mixed_res)
    ffn_in = (mixed_res * inv_two * gain_ffn).astype(BF)
    (ffn_all,) = communicate([Gather("fsdp", (T, W), BF, "both")], [ffn_in], 3)
    ffn_all = ffn_all.reshape(F * T, W)
    gate_pre = dot_nt(ffn_all, gate_proj)
    up_pre = dot_nt(ffn_all, up_proj)
    gate_sig = jax.nn.sigmoid(gate_pre)
    active = gate_pre * gate_sig
    hidden = (active * up_pre).astype(BF)
    d_hidden = dot_nt(dy_all, down_proj)
    d_gate = (d_hidden * up_pre * gate_sig * (1.0 + gate_pre * (1.0 - gate_sig))).astype(BF)
    d_up = (d_hidden * active).astype(BF)
    ffc = gate_proj.shape[0] // C
    grads = [
        dot_tn(a, b).astype(BF).reshape(CL, CD, ffc, W)
        for a, b in ((d_gate, ffn_all), (d_up, ffn_all), (hidden, dy_all))
    ]
    down_part = dot_nn(hidden, down_proj).astype(BF).reshape(L, D, T, W)
    back_part = (
        (dot_nn(d_gate, gate_proj) + dot_nn(d_up, up_proj)).astype(BF).reshape(L, D, T, W)
    )
    gate_grad, up_grad, down_grad, d_ffn_in, ffn_out = communicate(
        [
            Reduce("ctx", (ffc, W), BF),
            Reduce("ctx", (ffc, W), BF),
            Reduce("ctx", (ffc, W), BF),
            Reduce("fsdp", (T, W), BF, 4),
            Reduce("fsdp", (T, W), BF, 4, 0, 4),
        ],
        grads + [back_part, down_part],
        4,
    )
    block_output = (mixed_res + ffn_out).astype(BF)
    grad_gain_ffn = jnp.sum(d_ffn_in * mixed_res * inv_two, axis=0)
    d_mixed = out_cotangent.astype(F32) + norm_back(mixed_res, inv_two, gain_ffn, d_ffn_in)
    (dm_all,) = communicate([Gather("ctx", (T, W), BF, "line")], [d_mixed.astype(BF)], 5)
    dm_all = dm_all.reshape(G, W)
    d_local = dot_nt(dm_all, wo).astype(BF).reshape(G, hl, HEAD)
    row_delta = jnp.sum(d_local.astype(F32) * o_local.astype(F32), axis=2).T[:, :, None]
    d_prob = jnp.einsum("qhd,khd->hqk", d_local, v_local, preferred_element_type=F32)
    d_score = (prob_full * (d_prob - row_delta) * scale_att).astype(BF)
    dq_rot = jnp.einsum("hqk,khd->qhd", d_score, k_local, preferred_element_type=F32).astype(BF)
    dk_sum = jnp.einsum("hqk,qhd->khd", d_score, q_local, preferred_element_type=F32)
    dv_sum = jnp.einsum("hqk,qhd->khd", prob_bf, d_local, preferred_element_type=F32)
    dk_rot = jnp.sum(dk_sum.reshape(G, kl, share, HEAD), axis=2).astype(BF)
    d_values = jnp.sum(dv_sum.reshape(G, kl, share, HEAD), axis=2).astype(BF)
    d_q_norm = unrotate(dq_rot.astype(F32), cos_tab, sine_tab)
    d_k_norm = unrotate(dk_rot.astype(F32), cos_tab, sine_tab)
    grad_gain_q = jnp.sum(d_q_norm * queries * inv_query, axis=(0, 1))
    grad_gain_k = jnp.sum(d_k_norm * keys_raw * inv_key, axis=(0, 1))
    d_queries = norm_back(queries, inv_query, gain_query, d_q_norm).astype(BF).reshape(G, qw)
    d_keys = norm_back(keys_raw, inv_key, gain_key, d_k_norm).astype(BF).reshape(G, kw)
    d_qkv = jnp.concatenate([d_queries, d_keys, d_values.reshape(G, kw)], axis=1)
    dn_part = dot_nt(d_qkv, w_all).astype(BF).reshape(CL, CD, T, W)
    qkv_part = dot_tn(normed, d_qkv).astype(BF).reshape(L, D, rows, qw + 2 * kw)
    wo_part = dot_tn(o_flat, dm_all).astype(BF).reshape(L, D, qw // F, W)
    d_normed, qkv_sum, wo_sum = communicate(
        [
            Reduce("ctx", (T, W), BF),
            Reduce("fsdp", qkv_part.shape[2:], BF, 2, 0, 0, BF),
            Reduce("fsdp", wo_part.shape[2:], BF, 1, 1, 0, BF),
        ],
        [dn_part, qkv_part, wo_part],
        6,
    )
    grad_gain_attn = jnp.sum(d_normed * x_float * inv_one, axis=0)
    input_grad = d_mixed + norm_back(x_float, inv_one, gain_attn, d_normed)
    pair = jnp.concatenate([grad_gain_q, grad_gain_k])
    gains = jnp.concatenate(
        [
            jnp.pad(vec.reshape(F, 1, -1), ((0, 0), (0, 0), (0, 128 - vec.shape[0] // F)))
            for vec in (grad_gain_attn, grad_gain_ffn, pair)
        ]
        + [jnp.zeros((F, 5, 128), F32)],
        axis=1,
    )
    g_sum, query_grad, key_grad, value_grad, out_proj_grad = finish(
        gains, qkv_sum.reshape(C, rows // C, qw + 2 * kw), wo_sum, qw, kw, 7
    )
    return (
        block_output,
        input_grad,
        g_sum[0, :gain_w],
        query_grad,
        key_grad,
        value_grad,
        g_sum[2, :pair_w],
        out_proj_grad,
        g_sum[1, :gain_w],
        gate_grad,
        up_grad,
        down_grad,
    )


def solution(mesh):
    return jax.shard_map(
        on_device,
        mesh=mesh,
        in_specs=(
            P(("fsdp", "ctx"), None),
            P("fsdp"),
            P("fsdp", None),
            P("fsdp", None),
            P("fsdp", None),
            P("fsdp"),
            P("fsdp", None),
            P("fsdp"),
            P("fsdp", None),
            P("fsdp", None),
            P("fsdp", None),
            P("fsdp", None),
            P(("fsdp", "ctx"), None),
        ),
        out_specs=(
            P(("fsdp", "ctx"), None),
            P(("fsdp", "ctx"), None),
            P("fsdp"),
            P(("fsdp", "ctx"), None),
            P(("fsdp", "ctx"), None),
            P(("fsdp", "ctx"), None),
            P("fsdp"),
            P(("fsdp", "ctx"), None),
            P("fsdp"),
            P(("fsdp", "ctx"), None),
            P(("fsdp", "ctx"), None),
            P(("fsdp", "ctx"), None),
        ),
        check_vma=False,
    )
```

```python
import jax
import jax.numpy as jnp
from jax import lax
from jax.experimental import pallas as pl
from jax.experimental.pallas import tpu as pltpu
from jax.sharding import PartitionSpec as P

H = 16
KVH = 8
HEAD = 64


epsilon = 1e-05
rope_base = 1000000.0
masked_score = -1e30


def rms_scale(values):
    return lax.rsqrt(jnp.mean(values * values, axis=-1, keepdims=True) + epsilon)


def norm_back(values, inv_rms, gain_vec, upstream):
    scaled_up = upstream * gain_vec
    return inv_rms * scaled_up - values * (inv_rms * inv_rms * inv_rms) * jnp.mean(
        scaled_up * values, axis=-1, keepdims=True
    )


def segment_positions(lengths, token_count):
    seg_ends = jnp.cumsum(lengths)
    seg_starts = seg_ends - lengths
    token_index = jnp.arange(token_count, dtype=jnp.int32)
    segment = jnp.sum((token_index[:, None] >= seg_ends[None, :]).astype(jnp.int32), axis=1)
    seg_begin = jnp.max(
        jnp.where(token_index[:, None] >= seg_starts[None, :], seg_starts[None, :], 0), axis=1
    )
    return (segment, token_index - seg_begin)


def rope_tables(positions, head_width):
    half_width = head_width // 2
    frequency = rope_base ** (-(jnp.arange(half_width, dtype=jnp.float32) * 2.0 / head_width))
    angle_all = positions.astype(jnp.float32)[:, None] * frequency[None, :]
    return (jnp.cos(angle_all), jnp.sin(angle_all))


def rotate(values, cos_tab, sine_tab):
    half_width = values.shape[-1] // 2
    front_half = values[..., :half_width]
    back_half = values[..., half_width:]
    cos_b = cos_tab[:, None, :]
    sin_b = sine_tab[:, None, :]
    return jnp.concatenate(
        [front_half * cos_b - back_half * sin_b, back_half * cos_b + front_half * sin_b], axis=-1
    )


def unrotate(upstream, cos_tab, sine_tab):
    half_width = upstream.shape[-1] // 2
    front_half = upstream[..., :half_width]
    back_half = upstream[..., half_width:]
    cos_b = cos_tab[:, None, :]
    sin_b = sine_tab[:, None, :]
    return jnp.concatenate(
        [front_half * cos_b + back_half * sin_b, back_half * cos_b - front_half * sin_b], axis=-1
    )


def dot_nn(left_mat, right_mat):
    return jnp.dot(left_mat, right_mat, preferred_element_type=jnp.float32)


def dot_nt(left_mat, right_mat):
    return lax.dot_general(
        left_mat, right_mat, (((1,), (1,)), ((), ())), preferred_element_type=jnp.float32
    )


def dot_tn(left_mat, right_mat):
    return lax.dot_general(
        left_mat, right_mat, (((0,), (0,)), ((), ())), preferred_element_type=jnp.float32
    )


MESH = pl.DeviceIdType.MESH
BF = jnp.bfloat16
F32 = jnp.float32


def factor(name):
    count = lax.axis_size(name)
    if name == "ctx":
        direct = 2
    else:
        direct = 1
        while direct * direct * 4 <= count:
            direct *= 2
    return count // direct, direct


class Place:
    def __init__(self, name):
        self.name = name
        self.L, self.D = factor(name)
        index = lax.axis_index(name)
        self.l = index // self.D
        self.d = index % self.D

    def dev(self, l, d):
        return {self.name: l * self.D + d}

    def off(self, dd):
        return lax.rem(self.d + dd, self.D)


def remote(src, dst, ssem, rsem, dev):
    return pltpu.make_async_remote_copy(
        src_ref=src, dst_ref=dst, send_sem=ssem, recv_sem=rsem, device_id=dev, device_id_type=MESH
    )


def add_rows(dst, parts, lead):
    rows = dst.shape[-2]
    step = 16 if rows % 16 == 0 else rows

    def one(pick):
        def body(i, carry):
            at = pl.ds(pl.multiple_of(i * step, step), step) if step != rows else slice(None)
            if dst.dtype == BF and len(parts) == 2:
                pick(dst)[at, :] = pick(parts[0])[at, :] + pick(parts[1])[at, :]
                return carry
            total = pick(parts[0])[at, :].astype(F32)
            for part in parts[1:]:
                total = total + pick(part)[at, :].astype(F32)
            pick(dst)[at, :] = total.astype(dst.dtype)
            return carry

        if step == rows:
            body(0, 0)
        else:
            lax.fori_loop(0, rows // step, body, 0)

    if lead is None:
        one(lambda ref: ref)
    else:
        for j in range(lead):
            one(lambda ref, j=j: ref.at[j])


def line_neighbors(p, act):
    @pl.when(p.l > 0)
    def _():
        act(-1)

    @pl.when(p.l < p.L - 1)
    def _():
        act(1)


def pieces(rows, most):
    for count in range(most, 1, -1):
        if rows % (16 * count) == 0:
            return count
    return 1


def cut(first, rows, size):
    res = []
    while rows > 0:
        take = min(size, rows)
        res.append((first, take, "line"))
        first, rows = first + take, rows - take
    return res


class Gather:
    def __init__(self, name, shape, dtype, split):
        self.name, self.shape, self.dtype = name, shape, dtype
        self.L, self.D = factor(name)
        rows = shape[0]
        self.parts = []
        if split == "both":
            units = rows // 16
            lead = max(1, units // 8)
            self.parts = cut(0, rows - lead * 16, 32) + [(rows - lead * 16, lead * 16, "dir")]
        elif pieces(rows, 4) > 1:
            count = pieces(rows, 4)
            size = rows // count
            self.parts = [(i * size, size, split) for i in range(count)]
        else:
            self.parts = [(0, rows, split)]
        self.outs = [jax.ShapeDtypeStruct((self.L, self.D) + shape, dtype)]
        self.scratch = []
        dma = pltpu.SemaphoreType.DMA
        L, D = self.L, self.D
        for _, _, kind in self.parts:
            if kind == "line":
                self.scratch += [dma((2, L)), dma((L,)), dma((D, L)), dma((D, L))]
            else:
                self.scratch += [dma((D,)), dma((D,)), dma((D, 2, L)), dma((D, L))]

    def gens(self, p, ins, outs, scr):
        src, out = ins[0], outs[0]
        res = []
        for i, (r0, r, kind) in enumerate(self.parts):
            f = self.line_first if kind == "line" else self.dir_first
            res.append((0, f(p, src, out, r0, r, scr[4 * i : 4 * i + 4], i == 0)))
        return res

    def line_first(self, p, src, out, r0, r, sems, keep):
        ls, lr, ds, dr = sems
        L, D, l, d = p.L, p.D, p.l, p.d
        own = src.at[pl.ds(r0, r), :]

        def V(q, dd):
            return out.at[q, dd, pl.ds(r0, r), :]

        def line(q, dirn, view):
            return remote(view, V(q, d), ls.at[(dirn + 1) // 2, q], lr.at[q], p.dev(l + dirn, d))

        def direct(q, view, k):
            return remote(view, V(q, d), ds.at[k - 1, q], dr.at[k - 1, q], p.dev(l, p.off(k)))

        line_neighbors(p, lambda dirn: line(l, dirn, own).start())
        for k in range(1, D):
            direct(l, own, k).start()
        if keep:
            out[l, d] = src[...]
        yield
        for k in range(1, L):
            for sgn in (-1, 1):
                q = l + sgn * k

                @pl.when((q >= 0) & (q < L))
                def _(q=q, sgn=sgn):
                    line(q, -sgn, V(q, d)).wait_recv()
                    for m in range(1, D):
                        direct(q, V(q, d), m).start()

                    @pl.when((l - sgn >= 0) & (l - sgn < L))
                    def _():
                        line(q, -sgn, V(q, d)).start()

            yield
        for q in range(L):
            for k in range(1, D):
                w = V(q, p.off(D - k))
                remote(w, w, ds.at[k - 1, q], dr.at[k - 1, q], p.dev(l, p.off(k))).wait_recv()
        yield "drain"
        for q in range(L):
            for k in range(1, D):
                direct(q, V(q, d), k).wait_send()
        for k in range(0, L):
            for sgn in (-1, 1):
                if k == 0:
                    q = l

                    @pl.when((l - sgn >= 0) & (l - sgn < L))
                    def _(sgn=sgn):
                        line(l, -sgn, own).wait_send()
                else:
                    q = l + sgn * k

                    @pl.when((q >= 0) & (q < L) & (l - sgn >= 0) & (l - sgn < L))
                    def _(q=q, sgn=sgn):
                        line(q, -sgn, V(q, d)).wait_send()

    def dir_first(self, p, src, out, r0, r, sems, keep):
        ds, dr, ls, lr = sems
        L, D, l, d = p.L, p.D, p.l, p.d
        own = src.at[pl.ds(r0, r), :]

        def V(q, dd):
            return out.at[q, dd, pl.ds(r0, r), :]

        def line(j, q, dirn, view):
            return remote(
                view,
                V(q, p.off(D - j)),
                ls.at[j, (dirn + 1) // 2, q],
                lr.at[j, q],
                p.dev(l + dirn, d),
            )

        def direct(k):
            return remote(own, V(l, d), ds.at[k - 1], dr.at[k - 1], p.dev(l, p.off(k)))

        for k in range(1, D):
            direct(k).start()
        line_neighbors(p, lambda dirn: line(0, l, dirn, own).start())
        if keep:
            out[l, d] = src[...]
        yield
        for j in range(1, D):
            w = V(l, p.off(D - j))
            remote(w, w, ds.at[j - 1], dr.at[j - 1], p.dev(l, p.off(j))).wait_recv()
            line_neighbors(p, lambda dirn: line(j, l, dirn, w).start())
        yield
        for k in range(1, L):
            for j in range(D):
                for sgn in (-1, 1):
                    q = l + sgn * k

                    @pl.when((q >= 0) & (q < L))
                    def _(q=q, sgn=sgn, j=j):
                        w = V(q, p.off(D - j))
                        line(j, q, -sgn, w).wait_recv()

                        @pl.when((l - sgn >= 0) & (l - sgn < L))
                        def _():
                            line(j, q, -sgn, w).start()

            yield "drain" if k == L - 1 else None
        for k in range(1, D):
            direct(k).wait_send()
        for k in range(0, L):
            for j in range(D):
                for sgn in (-1, 1):
                    q = l + sgn * k if k else l

                    @pl.when((q >= 0) & (q < L) & (l - sgn >= 0) & (l - sgn < L))
                    def _(q=q, sgn=sgn, j=j):
                        line(j, q, -sgn, own if (k == 0 and j == 0) else V(q, p.off(D - j))).wait_send()


class Spread:
    def __init__(self, shape, dtype, chunks):
        self.shape, self.dtype, self.chunks = shape, dtype, chunks
        self.L, self.D = factor("fsdp")
        if lax.axis_size("ctx") != self.L:
            raise ValueError("unsupported mesh")
        self.name = "fsdp"
        self.outs = [jax.ShapeDtypeStruct((self.D,) + shape, dtype)]
        dma = pltpu.SemaphoreType.DMA
        self.scratch = [dma((chunks, 2)), dma((chunks,)), dma((chunks, self.D)), dma((chunks, self.D))]

    def gens(self, p, ins, outs, scr):
        rows = self.shape[0] // self.chunks
        return [(i, self.one(p, ins[0], outs[0], i, rows, scr)) for i in range(self.chunks)]

    def one(self, p, src, out, i, rows, scr):
        ls, lr, ds, dr = scr
        l, d, D = p.l, p.d, p.D
        c = lax.axis_index("ctx")
        own = src.at[pl.ds(i * rows, rows), :]
        at_home = l == c

        def V(dd):
            return out.at[dd, pl.ds(i * rows, rows), :]

        def line(dirn, view):
            return remote(view, V(d), ls.at[i, (dirn + 1) // 2], lr.at[i], p.dev(l + dirn, d))

        def direct(k, view):
            return remote(view, V(d), ds.at[i, k - 1], dr.at[i, k - 1], p.dev(l, p.off(k)))

        @pl.when(at_home)
        def _():
            line_neighbors(p, lambda dirn: line(dirn, own).start())
            for k in range(1, D):
                direct(k, own).start()
            if i == 0:
                out[d] = src[...]

        yield

        @pl.when(l > c)
        def _():
            line(1, V(d)).wait_recv()

            @pl.when(l < p.L - 1)
            def _():
                line(1, V(d)).start()

            for k in range(1, D):
                direct(k, V(d)).start()

        @pl.when(l < c)
        def _():
            line(-1, V(d)).wait_recv()

            @pl.when(l > 0)
            def _():
                line(-1, V(d)).start()

            for k in range(1, D):
                direct(k, V(d)).start()

        yield
        for k in range(1, D):
            w = V(p.off(D - k))
            remote(w, w, ds.at[i, k - 1], dr.at[i, k - 1], p.dev(l, p.off(k))).wait_recv()
        yield "drain"
        for k in range(1, D):
            direct(k, V(d)).wait_send()

        @pl.when((l <= c) & (l > 0))
        def _():
            line(-1, V(d)).wait_send()

        @pl.when((l >= c) & (l < p.L - 1))
        def _():
            line(1, V(d)).wait_send()


class Reduce:
    def __init__(self, name, shape, dtype, most=1, lines=0, first=0, result=F32):
        self.name, self.shape, self.dtype, self.first = name, shape, dtype, first
        self.L, self.D = factor(name)
        L, D = self.L, self.D
        self.outs = [jax.ShapeDtypeStruct(shape, result)]
        dma = pltpu.SemaphoreType.DMA
        self.count = pieces(shape[0], most if L * D <= 8 else min(most, 4))
        unit = (shape[0] // self.count,) + shape[1:]
        self.scratch = []
        self.kinds = ["dir"] * (self.count - lines) + ["line"] * min(lines, self.count)
        for kind in self.kinds:
            if kind == "line":
                self.scratch += [
                    pltpu.VMEM((L, D) + unit, dtype),
                    pltpu.VMEM((L, D) + unit, dtype),
                    pltpu.VMEM((D,) + unit, dtype),
                    pltpu.VMEM((max(D - 1, 1),) + unit, dtype),
                    dma((2, L)),
                    dma((2, L)),
                    dma((D,)),
                    dma((D,)),
                ]
            else:
                self.scratch += [
                    pltpu.VMEM((L,) + unit, dtype),
                    pltpu.VMEM((L,) + unit, dtype),
                    pltpu.VMEM((L,) + unit, dtype),
                    pltpu.VMEM((max(D - 1, 1), L) + unit, dtype),
                    dma((2, L)),
                    dma((2, L)),
                    dma((D, L)),
                    dma((D, L)),
                ]

    def gens(self, p, ins, outs, scr):
        size = self.shape[0] // self.count
        res = []
        for i, kind in enumerate(self.kinds):
            at = pl.ds(i * size, size)
            f = self.line_first if kind == "line" else self.dir_first
            start = 0 if kind == "line" else self.first + i
            res.append((start, f(p, ins[0], outs[0].at[at, :], at, scr[8 * i : 8 * i + 8])))
        return res

    def line_sum(self, p, own, from_left, from_right, ls, lr, lead, prep):
        L, l = p.L, p.l

        def right(q, view):
            return remote(view, from_left.at[q], ls.at[1, q], lr.at[1, q], p.dev(l + 1, p.d))

        def left(q, view):
            return remote(view, from_right.at[q], ls.at[0, q], lr.at[0, q], p.dev(l - 1, p.d))

        for t in range(L):
            qr, ql = L - 1 - t, t
            prep(qr)
            if qr > 0:

                @pl.when(l == 0)
                def _():
                    right(qr, own(qr)).start()

            prep(ql)
            if ql < L - 1:

                @pl.when(l == L - 1)
                def _():
                    left(ql, own(ql)).start()

        yield "late" if L <= 2 else None
        for k in range(1, L - 1):

            @pl.when(l == k)
            def _():
                for q in range(L - 1, k, -1):
                    right(q, from_left.at[q]).wait_recv()
                    add_rows(from_left.at[q], [from_left.at[q], own(q)], lead)
                    right(q, from_left.at[q]).start()

            @pl.when(l == L - 1 - k)
            def _():
                for q in range(L - 1 - k):
                    left(q, from_right.at[q]).wait_recv()
                    add_rows(from_right.at[q], [from_right.at[q], own(q)], lead)
                    left(q, from_right.at[q]).start()

            yield

    def line_total(self, p, own, from_left, from_right, ls, lr, dst, lead):
        l, L = p.l, p.L

        def arrive(way):
            v = (from_left if way == 1 else from_right).at[l]
            remote(v, v, ls.at[way, l], lr.at[way, l], p.dev(l + 1 - 2 * way, p.d)).wait_recv()

        @pl.when(l == 0)
        def _():
            arrive(0)
            add_rows(dst, [own(l), from_right.at[l]], lead)

        @pl.when(l == L - 1)
        def _():
            arrive(1)
            add_rows(dst, [own(l), from_left.at[l]], lead)

        if L > 2:

            @pl.when((l > 0) & (l < L - 1))
            def _():
                arrive(0)
                arrive(1)
                add_rows(dst, [own(l), from_left.at[l], from_right.at[l]], lead)

    def line_drain(self, p, from_left, from_right, ls, lr):
        L, l = p.L, p.l
        for q in range(L):
            if q > 0:

                @pl.when(l < q)
                def _():
                    v = from_left.at[q]
                    remote(v, v, ls.at[1, q], lr.at[1, q], p.dev(l + 1, p.d)).wait_send()

            if q < L - 1:

                @pl.when(l > q)
                def _():
                    v = from_right.at[q]
                    remote(v, v, ls.at[0, q], lr.at[0, q], p.dev(l - 1, p.d)).wait_send()

    def line_first(self, p, src, out, at, scr):
        from_left, from_right, acc, box, ls, lr, ds, dr = scr
        D, l, d = p.D, p.l, p.d

        def own(q):
            return src.at[q, :, at, :]

        yield from self.line_sum(p, own, from_left, from_right, ls, lr, D, lambda q: None)
        self.line_total(p, own, from_left, from_right, ls, lr, acc, D)

        def direct(k):
            return remote(
                acc.at[p.off(k)], box.at[k - 1], ds.at[k - 1], dr.at[k - 1], p.dev(l, p.off(k))
            )

        for k in range(1, D):
            direct(k).start()
        yield "late" if self.L > 2 else None
        for k in range(1, D):
            direct(k).wait_recv()
        add_rows(out, [acc.at[d]] + [box.at[k - 1] for k in range(1, D)], None)
        yield "drain"
        for k in range(1, D):
            direct(k).wait_send()
        self.line_drain(p, from_left, from_right, ls, lr)

    def dir_first(self, p, src, out, at, scr):
        from_left, from_right, acc, box, ls, lr, ds, dr = scr
        L, D, l, d = p.L, p.D, p.l, p.d

        def direct(k, q):
            return remote(
                src.at[q, p.off(k), at, :],
                box.at[k - 1, q],
                ds.at[k - 1, q],
                dr.at[k - 1, q],
                p.dev(l, p.off(k)),
            )

        order = []
        for t in range(L):
            for q in (L - 1 - t, t):
                if q not in order:
                    order.append(q)
        for q in order:
            for k in range(1, D):
                direct(k, q).start()
        yield
        ready = set()

        def prep(q):
            if q in ready:
                return
            ready.add(q)
            for k in range(1, D):
                direct(k, q).wait_recv()
            add_rows(
                acc.at[q], [src.at[q, d, at, :]] + [box.at[k - 1, q] for k in range(1, D)], None
            )

        def own(q):
            return acc.at[q]

        yield from self.line_sum(p, own, from_left, from_right, ls, lr, None, prep)
        self.line_total(p, own, from_left, from_right, ls, lr, out, None)
        yield "drain"
        for q in range(L):
            for k in range(1, D):
                direct(k, q).wait_send()
        self.line_drain(p, from_left, from_right, ls, lr)


def greet(places):
    barrier = pltpu.get_barrier_semaphore()
    count = 0
    for p in places:
        for k in range(1, p.D):
            pl.semaphore_signal(
                barrier, inc=1, device_id=p.dev(p.l, p.off(k)), device_id_type=MESH
            )
        count = count + (p.D - 1)
        line_neighbors(
            p,
            lambda dirn: pl.semaphore_signal(
                barrier, inc=1, device_id=p.dev(p.l + dirn, p.d), device_id_type=MESH
            ),
        )
        count = count + jnp.where(p.l > 0, 1, 0) + jnp.where(p.l < p.L - 1, 1, 0)
    pl.semaphore_wait(barrier, count)


def run_all(live):
    live = sorted(live, key=lambda pair: pair[0])
    late, drains, slot = [], [], 0
    while live:
        for start, g in live:
            if start == slot:
                next(g)
        rest = []
        for start, g in live:
            if start >= slot:
                rest.append((start, g))
                continue
            mark = next(g)
            if mark == "drain":
                drains.append(g)
            elif mark == "late":
                late.append(g)
            else:
                rest.append((start, g))
        live, slot = rest, slot + 1
    for g in late + drains:
        for _ in g:
            pass


def grant(items):
    total = 1 << 20
    for item in items:
        if item.dtype in (BF, F32):
            size = 2 if item.dtype == BF else 4
            for extent in item.shape:
                size *= extent
            total += size
    return total


def communicate(ops, arrays, cid):
    axes = sorted({op.name for op in ops})
    outs = [shape for op in ops for shape in op.outs]
    scratch = [s for op in ops for s in op.scratch]

    def kernel(*refs):
        ins = refs[: len(arrays)]
        out_refs = refs[len(arrays) : len(arrays) + len(outs)]
        scr = refs[len(arrays) + len(outs) :]
        places = {name: Place(name) for name in axes}
        greet([places[name] for name in axes])
        live = []
        o = s = 0
        for i, op in enumerate(ops):
            live += op.gens(
                places[op.name],
                [ins[i]],
                out_refs[o : o + len(op.outs)],
                scr[s : s + len(op.scratch)],
            )
            o += len(op.outs)
            s += len(op.scratch)
        run_all(live)

    vm = pl.BlockSpec(memory_space=pltpu.VMEM)
    return pl.pallas_call(
        kernel,
        out_shape=outs,
        in_specs=[vm] * len(arrays),
        out_specs=[vm] * len(outs),
        scratch_shapes=scratch,
        compiler_params=pltpu.CompilerParams(
            collective_id=cid,
            has_side_effects=True,
            vmem_limit_bytes=grant(list(arrays) + outs + scratch),
        ),
    )(*arrays)


def finish(gains, attn_piece, out_piece, qw, kw, cid):
    F, C = lax.axis_size("fsdp"), lax.axis_size("ctx")
    dma = pltpu.SemaphoreType.DMA

    def kernel(
        g, a, w, g_out, q_out, k_out, v_out, o_out,
        gbox, gsum, cbox, a_out, w_out, gs, gr, cs, cr, as_, ar, ws, wr
    ):
        f, c = lax.axis_index("fsdp"), lax.axis_index("ctx")
        goal = c * F + f
        gf, gc = goal // C, goal % C
        here = f * C + c
        sc, sf = here // F, here % F
        away = goal != here
        barrier = pltpu.get_barrier_semaphore()
        fpeer = [lax.rem(f + k, F) for k in range(F)]
        cpeer = [lax.rem(c + k, C) for k in range(C)]
        for k in range(1, F):
            pl.semaphore_signal(barrier, inc=1, device_id=(fpeer[k], c), device_id_type=MESH)
        for k in range(1, C):
            pl.semaphore_signal(barrier, inc=1, device_id=(f, cpeer[k]), device_id_type=MESH)

        @pl.when(away)
        def _():
            pl.semaphore_signal(barrier, inc=1, device_id=(sf, sc), device_id_type=MESH)

        pl.semaphore_wait(barrier, F + C - 2 + jnp.where(away, 1, 0))

        def gcopy(k):
            return remote(g.at[fpeer[k]], gbox.at[k - 1], gs.at[k], gr.at[k], (fpeer[k], c))

        def acopy(k):
            return remote(a.at[cpeer[k]], a_out.at[c], as_.at[k], ar.at[k], (f, cpeer[k]))

        def arecv(k):
            slot = a_out.at[lax.rem(c + C - k, C)]
            return remote(slot, slot, as_.at[k], ar.at[k], (f, cpeer[k]))

        def wcopy():
            return remote(w, w_out, ws.at[0], wr.at[0], (gf, gc))

        def ccopy(k):
            return remote(gsum, cbox.at[k - 1], cs.at[k], cr.at[k], (f, cpeer[k]))

        for k in range(1, F):
            gcopy(k).start()
        for k in range(1, C):
            acopy(k).start()

        @pl.when(away)
        def _():
            wcopy().start()

        @pl.when(jnp.logical_not(away))
        def _():
            w_out[...] = w[...]

        a_out[c] = a[c]
        total = g[f]
        for k in range(1, F):
            gcopy(k).wait_recv()
            total = total + gbox[k - 1]
        gsum[...] = total
        for k in range(1, C):
            ccopy(k).start()
        for k in range(1, C):
            ccopy(k).wait_recv()
            total = total + cbox[k - 1]
        g_out[...] = total
        for k in range(1, C):
            arecv(k).wait_recv()
        for s in range(C):
            q_out[:, s * qw : (s + 1) * qw] = a_out[s, :, :qw].astype(F32)
            k_out[:, s * kw : (s + 1) * kw] = a_out[s, :, qw : qw + kw].astype(F32)
            v_out[:, s * kw : (s + 1) * kw] = a_out[s, :, qw + kw :].astype(F32)
        for k in range(1, F):
            gcopy(k).wait_send()
        for k in range(1, C):
            acopy(k).wait_send()
            ccopy(k).wait_send()

        @pl.when(away)
        def _():
            wcopy().wait()

        o_out[...] = w_out[...].astype(F32)

    rows = attn_piece.shape[1]
    vm = pl.BlockSpec(memory_space=pltpu.VMEM)
    return pl.pallas_call(
        kernel,
        out_shape=[
            jax.ShapeDtypeStruct(gains.shape[1:], F32),
            jax.ShapeDtypeStruct((rows, C * qw), F32),
            jax.ShapeDtypeStruct((rows, C * kw), F32),
            jax.ShapeDtypeStruct((rows, C * kw), F32),
            jax.ShapeDtypeStruct(out_piece.shape, F32),
        ],
        in_specs=[vm] * 3,
        out_specs=[vm] * 5,
        scratch_shapes=[
            pltpu.VMEM((F - 1,) + gains.shape[1:], F32),
            pltpu.VMEM(gains.shape[1:], F32),
            pltpu.VMEM((C - 1,) + gains.shape[1:], F32),
            pltpu.VMEM(attn_piece.shape, attn_piece.dtype),
            pltpu.VMEM(out_piece.shape, out_piece.dtype),
        ]
        + [dma((F,)), dma((F,)), dma((C,)), dma((C,)), dma((C,)), dma((C,)), dma((1,)), dma((1,))],
        compiler_params=pltpu.CompilerParams(
            collective_id=cid, has_side_effects=True, vmem_limit_bytes=4 * 1024 * 1024
        ),
    )(gains, attn_piece, out_piece)


def emit(arrays):
    count = len(arrays)

    def kernel(*refs):
        sems = refs[2 * count]
        copies = [
            pltpu.make_async_copy(refs[i], refs[count + i], sems.at[i]) for i in range(count)
        ]
        for copy in copies:
            copy.start()
        for copy in copies:
            copy.wait()

    return pl.pallas_call(
        kernel,
        out_shape=[jax.ShapeDtypeStruct(a.shape, a.dtype) for a in arrays],
        in_specs=[pl.BlockSpec(memory_space=pltpu.VMEM)] * count,
        out_specs=[pl.BlockSpec(memory_space=pl.ANY)] * count,
        scratch_shapes=[pltpu.SemaphoreType.DMA((count,))],
        compiler_params=pltpu.CompilerParams(vmem_limit_bytes=8 * 1024 * 1024),
    )(*arrays)


def on_device(
    block_input,
    attn_gain,
    query_proj,
    key_proj,
    value_proj,
    qk_gain,
    out_proj,
    ffn_gain,
    gate_proj,
    up_proj,
    down_proj,
    seg_lengths,
    out_cotangent,
):
    T, W = block_input.shape
    C = lax.axis_size("ctx")
    F = lax.axis_size("fsdp")
    L, D = factor("fsdp")
    CL, CD = factor("ctx")
    G = T * C
    hl, kl, share = H // C, KVH // C, H // KVH
    qw, kw = hl * HEAD, kl * HEAD
    rows = query_proj.shape[0]
    scale_att = HEAD ** (-0.5)
    c = lax.axis_index("ctx")

    w_own = jnp.concatenate(
        [
            lax.dynamic_slice_in_dim(query_proj, c * qw, qw, axis=1),
            lax.dynamic_slice_in_dim(key_proj, c * kw, kw, axis=1),
            lax.dynamic_slice_in_dim(value_proj, c * kw, kw, axis=1),
        ],
        axis=1,
    )
    gain_w, pair_w = attn_gain.shape[0], qk_gain.shape[0]
    g_own = jnp.concatenate(
        [
            jnp.pad(vec[None, :], ((0, 0), (0, 128 - vec.shape[0])))
            for vec in (attn_gain, ffn_gain, qk_gain)
        ]
        + [jnp.zeros((13, 128), BF)],
        axis=0,
    )
    w_all, g_all, wo, x_all = communicate(
        [
            Gather("fsdp", w_own.shape, BF, "both"),
            Gather("fsdp", (16, 128), BF, "line"),
            Spread(out_proj.shape, BF, pieces(out_proj.shape[0], 4)),
            Gather("ctx", (T, W), BF, "line"),
        ],
        [w_own, g_own, out_proj, block_input],
        1,
    )
    x_all = x_all.reshape(G, W)
    w_all = w_all.reshape(W, qw + 2 * kw)
    wo = wo.reshape(qw, W)
    g_all = g_all.reshape(F, 16, 128)
    gain_attn = g_all[:, 0, :gain_w].reshape(W).astype(F32)
    gain_ffn = g_all[:, 1, :gain_w].reshape(W).astype(F32)
    gain_pair = g_all[:, 2, :pair_w].reshape(2 * HEAD).astype(F32)
    gain_query, gain_key = gain_pair[:HEAD], gain_pair[HEAD:]

    segment, positions = segment_positions(seg_lengths[0], G)
    cos_tab, sine_tab = rope_tables(positions, HEAD)
    xa = x_all.astype(F32)
    normed = (xa * rms_scale(xa) * gain_attn).astype(BF)
    qkv = dot_nn(normed, w_all)
    queries = qkv[:, :qw].reshape(G, hl, HEAD)
    keys_raw = qkv[:, qw : qw + kw].reshape(G, kl, HEAD)
    v_kv = qkv[:, qw + kw :].astype(BF).reshape(G, kl, HEAD)
    inv_query = rms_scale(queries)
    q_local = rotate(queries * inv_query * gain_query, cos_tab, sine_tab).astype(BF)
    inv_key = rms_scale(keys_raw)
    k_kv = rotate(keys_raw * inv_key * gain_key, cos_tab, sine_tab).astype(BF)
    k_local = jnp.repeat(k_kv, share, axis=1)
    v_local = jnp.repeat(v_kv, share, axis=1)
    token = jnp.arange(G, dtype=jnp.int32)
    allowed = (segment[:, None] == segment[None, :]) & (token[None, :] <= token[:, None])
    scores = (
        jnp.einsum("qhd,khd->hqk", q_local, k_local, preferred_element_type=F32) * scale_att
    )
    scores = jnp.where(allowed[None], scores, masked_score)
    top = jnp.max(scores, axis=2, keepdims=True)
    log_total = top + jnp.log(jnp.sum(jnp.exp(scores - top), axis=2, keepdims=True))
    prob_full = jnp.exp(scores - log_total)
    prob_bf = prob_full.astype(BF)
    o_local = jnp.einsum("hqk,khd->qhd", prob_bf, v_local, preferred_element_type=F32).astype(BF)
    o_flat = o_local.reshape(G, qw)
    part = dot_nn(o_flat, wo).astype(BF).reshape(CL, CD, T, W)
    attn_sum, dy_all = communicate(
        [Reduce("ctx", (T, W), BF, 2), Gather("fsdp", (T, W), BF, "both")],
        [part, out_cotangent],
        2,
    )
    dy_all = dy_all.reshape(F * T, W)

    x_float = block_input.astype(F32)
    inv_one = rms_scale(x_float)
    mixed_res = x_float + attn_sum
    inv_two = rms_scale(mixed_res)
    ffn_in = (mixed_res * inv_two * gain_ffn).astype(BF)
    (ffn_all,) = communicate([Gather("fsdp", (T, W), BF, "both")], [ffn_in], 3)
    ffn_all = ffn_all.reshape(F * T, W)
    gate_pre = dot_nt(ffn_all, gate_proj)
    up_pre = dot_nt(ffn_all, up_proj)
    gate_sig = jax.nn.sigmoid(gate_pre)
    active = gate_pre * gate_sig
    hidden = (active * up_pre).astype(BF)
    d_hidden = dot_nt(dy_all, down_proj)
    d_gate = (d_hidden * up_pre * gate_sig * (1.0 + gate_pre * (1.0 - gate_sig))).astype(BF)
    d_up = (d_hidden * active).astype(BF)
    ffc = gate_proj.shape[0] // C
    grads = [
        dot_tn(a, b).astype(BF).reshape(CL, CD, ffc, W)
        for a, b in ((d_gate, ffn_all), (d_up, ffn_all), (hidden, dy_all))
    ]
    down_part = dot_nn(hidden, down_proj).astype(BF).reshape(L, D, T, W)
    back_part = (
        (dot_nn(d_gate, gate_proj) + dot_nn(d_up, up_proj)).astype(BF).reshape(L, D, T, W)
    )
    gate_grad, up_grad, down_grad, d_ffn_in, ffn_out = communicate(
        [
            Reduce("ctx", (ffc, W), BF),
            Reduce("ctx", (ffc, W), BF),
            Reduce("ctx", (ffc, W), BF),
            Reduce("fsdp", (T, W), BF, 4),
            Reduce("fsdp", (T, W), BF, 4, 0, 4),
        ],
        grads + [back_part, down_part],
        4,
    )
    block_output = (mixed_res + ffn_out).astype(BF)
    grad_gain_ffn = jnp.sum(d_ffn_in * mixed_res * inv_two, axis=0)
    d_mixed = out_cotangent.astype(F32) + norm_back(mixed_res, inv_two, gain_ffn, d_ffn_in)
    (dm_all,) = communicate([Gather("ctx", (T, W), BF, "line")], [d_mixed.astype(BF)], 5)
    dm_all = dm_all.reshape(G, W)
    d_local = dot_nt(dm_all, wo).astype(BF).reshape(G, hl, HEAD)
    row_delta = jnp.sum(d_local.astype(F32) * o_local.astype(F32), axis=2).T[:, :, None]
    d_prob = jnp.einsum("qhd,khd->hqk", d_local, v_local, preferred_element_type=F32)
    d_score = (prob_full * (d_prob - row_delta) * scale_att).astype(BF)
    dq_rot = jnp.einsum("hqk,khd->qhd", d_score, k_local, preferred_element_type=F32).astype(BF)
    dk_sum = jnp.einsum("hqk,qhd->khd", d_score, q_local, preferred_element_type=F32)
    dv_sum = jnp.einsum("hqk,qhd->khd", prob_bf, d_local, preferred_element_type=F32)
    dk_rot = jnp.sum(dk_sum.reshape(G, kl, share, HEAD), axis=2).astype(BF)
    d_values = jnp.sum(dv_sum.reshape(G, kl, share, HEAD), axis=2).astype(BF)
    d_q_norm = unrotate(dq_rot.astype(F32), cos_tab, sine_tab)
    d_k_norm = unrotate(dk_rot.astype(F32), cos_tab, sine_tab)
    grad_gain_q = jnp.sum(d_q_norm * queries * inv_query, axis=(0, 1))
    grad_gain_k = jnp.sum(d_k_norm * keys_raw * inv_key, axis=(0, 1))
    d_queries = norm_back(queries, inv_query, gain_query, d_q_norm).astype(BF).reshape(G, qw)
    d_keys = norm_back(keys_raw, inv_key, gain_key, d_k_norm).astype(BF).reshape(G, kw)
    d_qkv = jnp.concatenate([d_queries, d_keys, d_values.reshape(G, kw)], axis=1)
    dn_part = dot_nt(d_qkv, w_all).astype(BF).reshape(CL, CD, T, W)
    qkv_part = dot_tn(normed, d_qkv).astype(BF).reshape(L, D, rows, qw + 2 * kw)
    wo_part = dot_tn(o_flat, dm_all).astype(BF).reshape(L, D, qw // F, W)
    d_normed, qkv_sum, wo_sum = communicate(
        [
            Reduce("ctx", (T, W), BF),
            Reduce("fsdp", qkv_part.shape[2:], BF, 2, 0, 0, BF),
            Reduce("fsdp", wo_part.shape[2:], BF, 1, 1, 0, BF),
        ],
        [dn_part, qkv_part, wo_part],
        6,
    )
    grad_gain_attn = jnp.sum(d_normed * x_float * inv_one, axis=0)
    input_grad = d_mixed + norm_back(x_float, inv_one, gain_attn, d_normed)
    pair = jnp.concatenate([grad_gain_q, grad_gain_k])
    gains = jnp.concatenate(
        [
            jnp.pad(vec.reshape(F, 1, -1), ((0, 0), (0, 0), (0, 128 - vec.shape[0] // F)))
            for vec in (grad_gain_attn, grad_gain_ffn, pair)
        ]
        + [jnp.zeros((F, 5, 128), F32)],
        axis=1,
    )
    g_sum, query_grad, key_grad, value_grad, out_proj_grad = finish(
        gains, qkv_sum.reshape(C, rows // C, qw + 2 * kw), wo_sum, qw, kw, 7
    )
    query_grad, key_grad, value_grad, out_proj_grad, gate_grad, up_grad, down_grad = emit(
        [query_grad, key_grad, value_grad, out_proj_grad, gate_grad, up_grad, down_grad]
    )
    return (
        block_output,
        input_grad,
        g_sum[0, :gain_w],
        query_grad,
        key_grad,
        value_grad,
        g_sum[2, :pair_w],
        out_proj_grad,
        g_sum[1, :gain_w],
        gate_grad,
        up_grad,
        down_grad,
    )


def solution(mesh):
    return jax.shard_map(
        on_device,
        mesh=mesh,
        in_specs=(
            P(("fsdp", "ctx"), None),
            P("fsdp"),
            P("fsdp", None),
            P("fsdp", None),
            P("fsdp", None),
            P("fsdp"),
            P("fsdp", None),
            P("fsdp"),
            P("fsdp", None),
            P("fsdp", None),
            P("fsdp", None),
            P("fsdp", None),
            P(("fsdp", "ctx"), None),
        ),
        out_specs=(
            P(("fsdp", "ctx"), None),
            P(("fsdp", "ctx"), None),
            P("fsdp"),
            P(("fsdp", "ctx"), None),
            P(("fsdp", "ctx"), None),
            P(("fsdp", "ctx"), None),
            P("fsdp"),
            P(("fsdp", "ctx"), None),
            P("fsdp"),
            P(("fsdp", "ctx"), None),
            P(("fsdp", "ctx"), None),
            P(("fsdp", "ctx"), None),
        ),
        check_vma=False,
    )
```

```python
import jax
import jax.numpy as jnp
from jax import lax
from jax.experimental import pallas as pl
from jax.experimental.pallas import tpu as pltpu
from jax.sharding import PartitionSpec as P

H = 16
KVH = 8
HEAD = 64


epsilon = 1e-05
rope_base = 1000000.0
masked_score = -1e30


def rms_scale(values):
    return lax.rsqrt(jnp.mean(values * values, axis=-1, keepdims=True) + epsilon)


def norm_back(values, inv_rms, gain_vec, upstream):
    scaled_up = upstream * gain_vec
    return inv_rms * scaled_up - values * (inv_rms * inv_rms * inv_rms) * jnp.mean(
        scaled_up * values, axis=-1, keepdims=True
    )


def segment_positions(lengths, token_count):
    seg_ends = jnp.cumsum(lengths)
    seg_starts = seg_ends - lengths
    token_index = jnp.arange(token_count, dtype=jnp.int32)
    segment = jnp.sum((token_index[:, None] >= seg_ends[None, :]).astype(jnp.int32), axis=1)
    seg_begin = jnp.max(
        jnp.where(token_index[:, None] >= seg_starts[None, :], seg_starts[None, :], 0), axis=1
    )
    return (segment, token_index - seg_begin)


def rope_tables(positions, head_width):
    half_width = head_width // 2
    frequency = rope_base ** (-(jnp.arange(half_width, dtype=jnp.float32) * 2.0 / head_width))
    angle_all = positions.astype(jnp.float32)[:, None] * frequency[None, :]
    return (jnp.cos(angle_all), jnp.sin(angle_all))


def rotate(values, cos_tab, sine_tab):
    half_width = values.shape[-1] // 2
    front_half = values[..., :half_width]
    back_half = values[..., half_width:]
    cos_b = cos_tab[:, None, :]
    sin_b = sine_tab[:, None, :]
    return jnp.concatenate(
        [front_half * cos_b - back_half * sin_b, back_half * cos_b + front_half * sin_b], axis=-1
    )


def unrotate(upstream, cos_tab, sine_tab):
    half_width = upstream.shape[-1] // 2
    front_half = upstream[..., :half_width]
    back_half = upstream[..., half_width:]
    cos_b = cos_tab[:, None, :]
    sin_b = sine_tab[:, None, :]
    return jnp.concatenate(
        [front_half * cos_b + back_half * sin_b, back_half * cos_b - front_half * sin_b], axis=-1
    )


def dot_nn(left_mat, right_mat):
    return jnp.dot(left_mat, right_mat, preferred_element_type=jnp.float32)


def dot_nt(left_mat, right_mat):
    return lax.dot_general(
        left_mat, right_mat, (((1,), (1,)), ((), ())), preferred_element_type=jnp.float32
    )


def dot_tn(left_mat, right_mat):
    return lax.dot_general(
        left_mat, right_mat, (((0,), (0,)), ((), ())), preferred_element_type=jnp.float32
    )


MESH = pl.DeviceIdType.MESH
BF = jnp.bfloat16
F32 = jnp.float32


def factor(name):
    count = lax.axis_size(name)
    if name == "ctx":
        direct = 2
    else:
        direct = 1
        while direct * direct * 4 <= count:
            direct *= 2
    return count // direct, direct


class Place:
    def __init__(self, name):
        self.name = name
        self.L, self.D = factor(name)
        index = lax.axis_index(name)
        self.l = index // self.D
        self.d = index % self.D

    def dev(self, l, d):
        return {self.name: l * self.D + d}

    def off(self, dd):
        return lax.rem(self.d + dd, self.D)


def remote(src, dst, ssem, rsem, dev):
    return pltpu.make_async_remote_copy(
        src_ref=src, dst_ref=dst, send_sem=ssem, recv_sem=rsem, device_id=dev, device_id_type=MESH
    )


def add_rows(dst, parts, lead):
    rows = dst.shape[-2]
    step = 16 if rows % 16 == 0 else rows

    def one(pick):
        def body(i, carry):
            at = pl.ds(pl.multiple_of(i * step, step), step) if step != rows else slice(None)
            if dst.dtype == BF and len(parts) == 2:
                pick(dst)[at, :] = pick(parts[0])[at, :] + pick(parts[1])[at, :]
                return carry
            total = pick(parts[0])[at, :].astype(F32)
            for part in parts[1:]:
                total = total + pick(part)[at, :].astype(F32)
            pick(dst)[at, :] = total.astype(dst.dtype)
            return carry

        if step == rows:
            body(0, 0)
        else:
            lax.fori_loop(0, rows // step, body, 0)

    if lead is None:
        one(lambda ref: ref)
    else:
        for j in range(lead):
            one(lambda ref, j=j: ref.at[j])


def line_neighbors(p, act):
    @pl.when(p.l > 0)
    def _():
        act(-1)

    @pl.when(p.l < p.L - 1)
    def _():
        act(1)


def pieces(rows, most):
    for count in range(most, 1, -1):
        if rows % (16 * count) == 0:
            return count
    return 1


def cut(first, rows, size):
    res = []
    while rows > 0:
        take = min(size, rows)
        res.append((first, take, "line"))
        first, rows = first + take, rows - take
    return res


class Gather:
    def __init__(self, name, shape, dtype, split):
        self.name, self.shape, self.dtype = name, shape, dtype
        self.L, self.D = factor(name)
        rows = shape[0]
        self.parts = []
        if split == "both":
            units = rows // 16
            lead = max(1, units // 8)
            self.parts = cut(0, rows - lead * 16, 32) + [(rows - lead * 16, lead * 16, "dir")]
        elif pieces(rows, 4) > 1:
            count = pieces(rows, 4)
            size = rows // count
            self.parts = [(i * size, size, split) for i in range(count)]
        else:
            self.parts = [(0, rows, split)]
        self.outs = [jax.ShapeDtypeStruct((self.L, self.D) + shape, dtype)]
        self.scratch = []
        dma = pltpu.SemaphoreType.DMA
        L, D = self.L, self.D
        for _, _, kind in self.parts:
            if kind == "line":
                self.scratch += [dma((2, L)), dma((L,)), dma((D, L)), dma((D, L))]
            else:
                self.scratch += [dma((D,)), dma((D,)), dma((D, 2, L)), dma((D, L))]

    def gens(self, p, ins, outs, scr):
        src, out = ins[0], outs[0]
        res = []
        for i, (r0, r, kind) in enumerate(self.parts):
            f = self.line_first if kind == "line" else self.dir_first
            res.append((0, f(p, src, out, r0, r, scr[4 * i : 4 * i + 4], i == 0)))
        return res

    def line_first(self, p, src, out, r0, r, sems, keep):
        ls, lr, ds, dr = sems
        L, D, l, d = p.L, p.D, p.l, p.d
        own = src.at[pl.ds(r0, r), :]

        def V(q, dd):
            return out.at[q, dd, pl.ds(r0, r), :]

        def line(q, dirn, view):
            return remote(view, V(q, d), ls.at[(dirn + 1) // 2, q], lr.at[q], p.dev(l + dirn, d))

        def direct(q, view, k):
            return remote(view, V(q, d), ds.at[k - 1, q], dr.at[k - 1, q], p.dev(l, p.off(k)))

        line_neighbors(p, lambda dirn: line(l, dirn, own).start())
        for k in range(1, D):
            direct(l, own, k).start()
        if keep:
            out[l, d] = src[...]
        yield
        for k in range(1, L):
            for sgn in (-1, 1):
                q = l + sgn * k

                @pl.when((q >= 0) & (q < L))
                def _(q=q, sgn=sgn):
                    line(q, -sgn, V(q, d)).wait_recv()
                    for m in range(1, D):
                        direct(q, V(q, d), m).start()

                    @pl.when((l - sgn >= 0) & (l - sgn < L))
                    def _():
                        line(q, -sgn, V(q, d)).start()

            yield
        for q in range(L):
            for k in range(1, D):
                w = V(q, p.off(D - k))
                remote(w, w, ds.at[k - 1, q], dr.at[k - 1, q], p.dev(l, p.off(k))).wait_recv()
        yield "drain"
        for q in range(L):
            for k in range(1, D):
                direct(q, V(q, d), k).wait_send()
        for k in range(0, L):
            for sgn in (-1, 1):
                if k == 0:
                    q = l

                    @pl.when((l - sgn >= 0) & (l - sgn < L))
                    def _(sgn=sgn):
                        line(l, -sgn, own).wait_send()
                else:
                    q = l + sgn * k

                    @pl.when((q >= 0) & (q < L) & (l - sgn >= 0) & (l - sgn < L))
                    def _(q=q, sgn=sgn):
                        line(q, -sgn, V(q, d)).wait_send()

    def dir_first(self, p, src, out, r0, r, sems, keep):
        ds, dr, ls, lr = sems
        L, D, l, d = p.L, p.D, p.l, p.d
        own = src.at[pl.ds(r0, r), :]

        def V(q, dd):
            return out.at[q, dd, pl.ds(r0, r), :]

        def line(j, q, dirn, view):
            return remote(
                view,
                V(q, p.off(D - j)),
                ls.at[j, (dirn + 1) // 2, q],
                lr.at[j, q],
                p.dev(l + dirn, d),
            )

        def direct(k):
            return remote(own, V(l, d), ds.at[k - 1], dr.at[k - 1], p.dev(l, p.off(k)))

        for k in range(1, D):
            direct(k).start()
        line_neighbors(p, lambda dirn: line(0, l, dirn, own).start())
        if keep:
            out[l, d] = src[...]
        yield
        for j in range(1, D):
            w = V(l, p.off(D - j))
            remote(w, w, ds.at[j - 1], dr.at[j - 1], p.dev(l, p.off(j))).wait_recv()
            line_neighbors(p, lambda dirn: line(j, l, dirn, w).start())
        yield
        for k in range(1, L):
            for j in range(D):
                for sgn in (-1, 1):
                    q = l + sgn * k

                    @pl.when((q >= 0) & (q < L))
                    def _(q=q, sgn=sgn, j=j):
                        w = V(q, p.off(D - j))
                        line(j, q, -sgn, w).wait_recv()

                        @pl.when((l - sgn >= 0) & (l - sgn < L))
                        def _():
                            line(j, q, -sgn, w).start()

            yield "drain" if k == L - 1 else None
        for k in range(1, D):
            direct(k).wait_send()
        for k in range(0, L):
            for j in range(D):
                for sgn in (-1, 1):
                    q = l + sgn * k if k else l

                    @pl.when((q >= 0) & (q < L) & (l - sgn >= 0) & (l - sgn < L))
                    def _(q=q, sgn=sgn, j=j):
                        line(j, q, -sgn, own if (k == 0 and j == 0) else V(q, p.off(D - j))).wait_send()


class Spread:
    def __init__(self, shape, dtype, chunks):
        self.shape, self.dtype, self.chunks = shape, dtype, chunks
        self.L, self.D = factor("fsdp")
        if lax.axis_size("ctx") != self.L:
            raise ValueError("unsupported mesh")
        self.name = "fsdp"
        self.outs = [jax.ShapeDtypeStruct((self.D,) + shape, dtype)]
        dma = pltpu.SemaphoreType.DMA
        self.scratch = [dma((chunks, 2)), dma((chunks,)), dma((chunks, self.D)), dma((chunks, self.D))]

    def gens(self, p, ins, outs, scr):
        rows = self.shape[0] // self.chunks
        return [(i, self.one(p, ins[0], outs[0], i, rows, scr)) for i in range(self.chunks)]

    def one(self, p, src, out, i, rows, scr):
        ls, lr, ds, dr = scr
        l, d, D = p.l, p.d, p.D
        c = lax.axis_index("ctx")
        own = src.at[pl.ds(i * rows, rows), :]
        at_home = l == c

        def V(dd):
            return out.at[dd, pl.ds(i * rows, rows), :]

        def line(dirn, view):
            return remote(view, V(d), ls.at[i, (dirn + 1) // 2], lr.at[i], p.dev(l + dirn, d))

        def direct(k, view):
            return remote(view, V(d), ds.at[i, k - 1], dr.at[i, k - 1], p.dev(l, p.off(k)))

        @pl.when(at_home)
        def _():
            line_neighbors(p, lambda dirn: line(dirn, own).start())
            for k in range(1, D):
                direct(k, own).start()
            if i == 0:
                out[d] = src[...]

        yield

        @pl.when(l > c)
        def _():
            line(1, V(d)).wait_recv()

            @pl.when(l < p.L - 1)
            def _():
                line(1, V(d)).start()

            for k in range(1, D):
                direct(k, V(d)).start()

        @pl.when(l < c)
        def _():
            line(-1, V(d)).wait_recv()

            @pl.when(l > 0)
            def _():
                line(-1, V(d)).start()

            for k in range(1, D):
                direct(k, V(d)).start()

        yield
        for k in range(1, D):
            w = V(p.off(D - k))
            remote(w, w, ds.at[i, k - 1], dr.at[i, k - 1], p.dev(l, p.off(k))).wait_recv()
        yield "drain"
        for k in range(1, D):
            direct(k, V(d)).wait_send()

        @pl.when((l <= c) & (l > 0))
        def _():
            line(-1, V(d)).wait_send()

        @pl.when((l >= c) & (l < p.L - 1))
        def _():
            line(1, V(d)).wait_send()


class Reduce:
    def __init__(self, name, shape, dtype, most=1, lines=0, first=0, result=F32):
        self.name, self.shape, self.dtype, self.first = name, shape, dtype, first
        self.L, self.D = factor(name)
        L, D = self.L, self.D
        self.outs = [jax.ShapeDtypeStruct(shape, result)]
        dma = pltpu.SemaphoreType.DMA
        self.count = pieces(shape[0], most if L * D <= 8 else min(most, 4))
        unit = (shape[0] // self.count,) + shape[1:]
        self.scratch = []
        self.kinds = ["dir"] * (self.count - lines) + ["line"] * min(lines, self.count)
        for kind in self.kinds:
            if kind == "line":
                self.scratch += [
                    pltpu.VMEM((L, D) + unit, dtype),
                    pltpu.VMEM((L, D) + unit, dtype),
                    pltpu.VMEM((D,) + unit, dtype),
                    pltpu.VMEM((max(D - 1, 1),) + unit, dtype),
                    dma((2, L)),
                    dma((2, L)),
                    dma((D,)),
                    dma((D,)),
                ]
            else:
                self.scratch += [
                    pltpu.VMEM((L,) + unit, dtype),
                    pltpu.VMEM((L,) + unit, dtype),
                    pltpu.VMEM((L,) + unit, dtype),
                    pltpu.VMEM((max(D - 1, 1), L) + unit, dtype),
                    dma((2, L)),
                    dma((2, L)),
                    dma((D, L)),
                    dma((D, L)),
                ]

    def gens(self, p, ins, outs, scr):
        size = self.shape[0] // self.count
        res = []
        for i, kind in enumerate(self.kinds):
            at = pl.ds(i * size, size)
            f = self.line_first if kind == "line" else self.dir_first
            start = 0 if kind == "line" else self.first + i
            res.append((start, f(p, ins[0], outs[0].at[at, :], at, scr[8 * i : 8 * i + 8])))
        return res

    def line_sum(self, p, own, from_left, from_right, ls, lr, lead, prep):
        L, l = p.L, p.l

        def right(q, view):
            return remote(view, from_left.at[q], ls.at[1, q], lr.at[1, q], p.dev(l + 1, p.d))

        def left(q, view):
            return remote(view, from_right.at[q], ls.at[0, q], lr.at[0, q], p.dev(l - 1, p.d))

        for t in range(L):
            qr, ql = L - 1 - t, t
            prep(qr)
            if qr > 0:

                @pl.when(l == 0)
                def _():
                    right(qr, own(qr)).start()

            prep(ql)
            if ql < L - 1:

                @pl.when(l == L - 1)
                def _():
                    left(ql, own(ql)).start()

        yield "late" if L <= 2 else None
        for k in range(1, L - 1):

            @pl.when(l == k)
            def _():
                for q in range(L - 1, k, -1):
                    right(q, from_left.at[q]).wait_recv()
                    add_rows(from_left.at[q], [from_left.at[q], own(q)], lead)
                    right(q, from_left.at[q]).start()

            @pl.when(l == L - 1 - k)
            def _():
                for q in range(L - 1 - k):
                    left(q, from_right.at[q]).wait_recv()
                    add_rows(from_right.at[q], [from_right.at[q], own(q)], lead)
                    left(q, from_right.at[q]).start()

            yield

    def line_total(self, p, own, from_left, from_right, ls, lr, dst, lead):
        l, L = p.l, p.L

        def arrive(way):
            v = (from_left if way == 1 else from_right).at[l]
            remote(v, v, ls.at[way, l], lr.at[way, l], p.dev(l + 1 - 2 * way, p.d)).wait_recv()

        @pl.when(l == 0)
        def _():
            arrive(0)
            add_rows(dst, [own(l), from_right.at[l]], lead)

        @pl.when(l == L - 1)
        def _():
            arrive(1)
            add_rows(dst, [own(l), from_left.at[l]], lead)

        if L > 2:

            @pl.when((l > 0) & (l < L - 1))
            def _():
                arrive(0)
                arrive(1)
                add_rows(dst, [own(l), from_left.at[l], from_right.at[l]], lead)

    def line_drain(self, p, from_left, from_right, ls, lr):
        L, l = p.L, p.l
        for q in range(L):
            if q > 0:

                @pl.when(l < q)
                def _():
                    v = from_left.at[q]
                    remote(v, v, ls.at[1, q], lr.at[1, q], p.dev(l + 1, p.d)).wait_send()

            if q < L - 1:

                @pl.when(l > q)
                def _():
                    v = from_right.at[q]
                    remote(v, v, ls.at[0, q], lr.at[0, q], p.dev(l - 1, p.d)).wait_send()

    def line_first(self, p, src, out, at, scr):
        from_left, from_right, acc, box, ls, lr, ds, dr = scr
        D, l, d = p.D, p.l, p.d

        def own(q):
            return src.at[q, :, at, :]

        yield from self.line_sum(p, own, from_left, from_right, ls, lr, D, lambda q: None)
        self.line_total(p, own, from_left, from_right, ls, lr, acc, D)

        def direct(k):
            return remote(
                acc.at[p.off(k)], box.at[k - 1], ds.at[k - 1], dr.at[k - 1], p.dev(l, p.off(k))
            )

        for k in range(1, D):
            direct(k).start()
        yield "late" if self.L > 2 else None
        for k in range(1, D):
            direct(k).wait_recv()
        add_rows(out, [acc.at[d]] + [box.at[k - 1] for k in range(1, D)], None)
        yield "drain"
        for k in range(1, D):
            direct(k).wait_send()
        self.line_drain(p, from_left, from_right, ls, lr)

    def dir_first(self, p, src, out, at, scr):
        from_left, from_right, acc, box, ls, lr, ds, dr = scr
        L, D, l, d = p.L, p.D, p.l, p.d

        def direct(k, q):
            return remote(
                src.at[q, p.off(k), at, :],
                box.at[k - 1, q],
                ds.at[k - 1, q],
                dr.at[k - 1, q],
                p.dev(l, p.off(k)),
            )

        order = []
        for t in range(L):
            for q in (L - 1 - t, t):
                if q not in order:
                    order.append(q)
        for q in order:
            for k in range(1, D):
                direct(k, q).start()
        yield
        ready = set()

        def prep(q):
            if q in ready:
                return
            ready.add(q)
            for k in range(1, D):
                direct(k, q).wait_recv()
            add_rows(
                acc.at[q], [src.at[q, d, at, :]] + [box.at[k - 1, q] for k in range(1, D)], None
            )

        def own(q):
            return acc.at[q]

        yield from self.line_sum(p, own, from_left, from_right, ls, lr, None, prep)
        self.line_total(p, own, from_left, from_right, ls, lr, out, None)
        yield "drain"
        for q in range(L):
            for k in range(1, D):
                direct(k, q).wait_send()
        self.line_drain(p, from_left, from_right, ls, lr)


def greet(places):
    barrier = pltpu.get_barrier_semaphore()
    count = 0
    for p in places:
        for k in range(1, p.D):
            pl.semaphore_signal(
                barrier, inc=1, device_id=p.dev(p.l, p.off(k)), device_id_type=MESH
            )
        count = count + (p.D - 1)
        line_neighbors(
            p,
            lambda dirn: pl.semaphore_signal(
                barrier, inc=1, device_id=p.dev(p.l + dirn, p.d), device_id_type=MESH
            ),
        )
        count = count + jnp.where(p.l > 0, 1, 0) + jnp.where(p.l < p.L - 1, 1, 0)
    pl.semaphore_wait(barrier, count)


def run_all(live):
    live = sorted(live, key=lambda pair: pair[0])
    late, drains, slot = [], [], 0
    while live:
        for start, g in live:
            if start == slot:
                next(g)
        rest = []
        for start, g in live:
            if start >= slot:
                rest.append((start, g))
                continue
            mark = next(g)
            if mark == "drain":
                drains.append(g)
            elif mark == "late":
                late.append(g)
            else:
                rest.append((start, g))
        live, slot = rest, slot + 1
    for g in late + drains:
        for _ in g:
            pass


def grant(items):
    total = 1 << 20
    for item in items:
        if item.dtype in (BF, F32):
            size = 2 if item.dtype == BF else 4
            for extent in item.shape:
                size *= extent
            total += size
    return total


def communicate(ops, arrays, cid):
    axes = sorted({op.name for op in ops})
    outs = [shape for op in ops for shape in op.outs]
    scratch = [s for op in ops for s in op.scratch]

    def kernel(*refs):
        ins = refs[: len(arrays)]
        out_refs = refs[len(arrays) : len(arrays) + len(outs)]
        scr = refs[len(arrays) + len(outs) :]
        places = {name: Place(name) for name in axes}
        greet([places[name] for name in axes])
        live = []
        o = s = 0
        for i, op in enumerate(ops):
            live += op.gens(
                places[op.name],
                [ins[i]],
                out_refs[o : o + len(op.outs)],
                scr[s : s + len(op.scratch)],
            )
            o += len(op.outs)
            s += len(op.scratch)
        run_all(live)

    vm = pl.BlockSpec(memory_space=pltpu.VMEM)
    return pl.pallas_call(
        kernel,
        out_shape=outs,
        in_specs=[vm] * len(arrays),
        out_specs=[vm] * len(outs),
        scratch_shapes=scratch,
        compiler_params=pltpu.CompilerParams(
            collective_id=cid,
            has_side_effects=True,
            vmem_limit_bytes=grant(list(arrays) + outs + scratch),
        ),
    )(*arrays)


def finish(gains, attn_piece, out_piece, qw, kw, cid):
    F, C = lax.axis_size("fsdp"), lax.axis_size("ctx")
    dma = pltpu.SemaphoreType.DMA

    def kernel(
        g, a, w, g_out, q_out, k_out, v_out, o_out,
        gbox, gsum, cbox, a_out, w_out, gs, gr, cs, cr, as_, ar, ws, wr
    ):
        f, c = lax.axis_index("fsdp"), lax.axis_index("ctx")
        goal = c * F + f
        gf, gc = goal // C, goal % C
        here = f * C + c
        sc, sf = here // F, here % F
        away = goal != here
        barrier = pltpu.get_barrier_semaphore()
        fpeer = [lax.rem(f + k, F) for k in range(F)]
        cpeer = [lax.rem(c + k, C) for k in range(C)]
        for k in range(1, F):
            pl.semaphore_signal(barrier, inc=1, device_id=(fpeer[k], c), device_id_type=MESH)
        for k in range(1, C):
            pl.semaphore_signal(barrier, inc=1, device_id=(f, cpeer[k]), device_id_type=MESH)

        @pl.when(away)
        def _():
            pl.semaphore_signal(barrier, inc=1, device_id=(sf, sc), device_id_type=MESH)

        pl.semaphore_wait(barrier, F + C - 2 + jnp.where(away, 1, 0))

        def gcopy(k):
            return remote(g.at[fpeer[k]], gbox.at[k - 1], gs.at[k], gr.at[k], (fpeer[k], c))

        def acopy(k):
            return remote(a.at[cpeer[k]], a_out.at[c], as_.at[k], ar.at[k], (f, cpeer[k]))

        def arecv(k):
            slot = a_out.at[lax.rem(c + C - k, C)]
            return remote(slot, slot, as_.at[k], ar.at[k], (f, cpeer[k]))

        def wcopy():
            return remote(w, w_out, ws.at[0], wr.at[0], (gf, gc))

        def ccopy(k):
            return remote(gsum, cbox.at[k - 1], cs.at[k], cr.at[k], (f, cpeer[k]))

        for k in range(1, F):
            gcopy(k).start()
        for k in range(1, C):
            acopy(k).start()

        @pl.when(away)
        def _():
            wcopy().start()

        @pl.when(jnp.logical_not(away))
        def _():
            w_out[...] = w[...]

        a_out[c] = a[c]
        total = g[f]
        for k in range(1, F):
            gcopy(k).wait_recv()
            total = total + gbox[k - 1]
        gsum[...] = total
        for k in range(1, C):
            ccopy(k).start()
        for k in range(1, C):
            ccopy(k).wait_recv()
            total = total + cbox[k - 1]
        g_out[...] = total
        for k in range(1, C):
            arecv(k).wait_recv()
        for s in range(C):
            q_out[:, s * qw : (s + 1) * qw] = a_out[s, :, :qw].astype(F32)
            k_out[:, s * kw : (s + 1) * kw] = a_out[s, :, qw : qw + kw].astype(F32)
            v_out[:, s * kw : (s + 1) * kw] = a_out[s, :, qw + kw :].astype(F32)
        for k in range(1, F):
            gcopy(k).wait_send()
        for k in range(1, C):
            acopy(k).wait_send()
            ccopy(k).wait_send()

        @pl.when(away)
        def _():
            wcopy().wait()

        o_out[...] = w_out[...].astype(F32)

    rows = attn_piece.shape[1]
    vm = pl.BlockSpec(memory_space=pltpu.VMEM)
    return pl.pallas_call(
        kernel,
        out_shape=[
            jax.ShapeDtypeStruct(gains.shape[1:], F32),
            jax.ShapeDtypeStruct((rows, C * qw), F32),
            jax.ShapeDtypeStruct((rows, C * kw), F32),
            jax.ShapeDtypeStruct((rows, C * kw), F32),
            jax.ShapeDtypeStruct(out_piece.shape, F32),
        ],
        in_specs=[vm] * 3,
        out_specs=[vm] * 5,
        scratch_shapes=[
            pltpu.VMEM((F - 1,) + gains.shape[1:], F32),
            pltpu.VMEM(gains.shape[1:], F32),
            pltpu.VMEM((C - 1,) + gains.shape[1:], F32),
            pltpu.VMEM(attn_piece.shape, attn_piece.dtype),
            pltpu.VMEM(out_piece.shape, out_piece.dtype),
        ]
        + [dma((F,)), dma((F,)), dma((C,)), dma((C,)), dma((C,)), dma((C,)), dma((1,)), dma((1,))],
        compiler_params=pltpu.CompilerParams(
            collective_id=cid, has_side_effects=True, vmem_limit_bytes=4 * 1024 * 1024
        ),
    )(gains, attn_piece, out_piece)


def emit(arrays):
    count = len(arrays)

    def kernel(*refs):
        sems = refs[2 * count]
        copies = [
            pltpu.make_async_copy(refs[i], refs[count + i], sems.at[i]) for i in range(count)
        ]
        for copy in copies:
            copy.start()
        for copy in copies:
            copy.wait()

    return pl.pallas_call(
        kernel,
        out_shape=[jax.ShapeDtypeStruct(a.shape, a.dtype) for a in arrays],
        in_specs=[pl.BlockSpec(memory_space=pltpu.VMEM)] * count,
        out_specs=[pl.BlockSpec(memory_space=pl.ANY)] * count,
        scratch_shapes=[pltpu.SemaphoreType.DMA((count,))],
        compiler_params=pltpu.CompilerParams(vmem_limit_bytes=8 * 1024 * 1024),
    )(*arrays)


def on_device(
    block_input,
    attn_gain,
    query_proj,
    key_proj,
    value_proj,
    qk_gain,
    out_proj,
    ffn_gain,
    gate_proj,
    up_proj,
    down_proj,
    seg_lengths,
    out_cotangent,
):
    T, W = block_input.shape
    C = lax.axis_size("ctx")
    F = lax.axis_size("fsdp")
    L, D = factor("fsdp")
    CL, CD = factor("ctx")
    G = T * C
    hl, kl, share = H // C, KVH // C, H // KVH
    qw, kw = hl * HEAD, kl * HEAD
    rows = query_proj.shape[0]
    scale_att = HEAD ** (-0.5)
    c = lax.axis_index("ctx")

    w_own = jnp.concatenate(
        [
            lax.dynamic_slice_in_dim(query_proj, c * qw, qw, axis=1),
            lax.dynamic_slice_in_dim(key_proj, c * kw, kw, axis=1),
            lax.dynamic_slice_in_dim(value_proj, c * kw, kw, axis=1),
        ],
        axis=1,
    )
    gain_w, pair_w = attn_gain.shape[0], qk_gain.shape[0]
    g_own = jnp.concatenate(
        [
            jnp.pad(vec[None, :], ((0, 0), (0, 128 - vec.shape[0])))
            for vec in (attn_gain, ffn_gain, qk_gain)
        ]
        + [jnp.zeros((13, 128), BF)],
        axis=0,
    )
    w_all, g_all, wo, x_all = communicate(
        [
            Gather("fsdp", w_own.shape, BF, "both"),
            Gather("fsdp", (16, 128), BF, "line"),
            Spread(out_proj.shape, BF, pieces(out_proj.shape[0], 4)),
            Gather("ctx", (T, W), BF, "line"),
        ],
        [w_own, g_own, out_proj, block_input],
        1,
    )
    x_all = x_all.reshape(G, W)
    w_all = w_all.reshape(W, qw + 2 * kw)
    wo = wo.reshape(qw, W)
    g_all = g_all.reshape(F, 16, 128)
    gain_attn = g_all[:, 0, :gain_w].reshape(W).astype(F32)
    gain_ffn = g_all[:, 1, :gain_w].reshape(W).astype(F32)
    gain_pair = g_all[:, 2, :pair_w].reshape(2 * HEAD).astype(F32)
    gain_query, gain_key = gain_pair[:HEAD], gain_pair[HEAD:]

    segment, positions = segment_positions(seg_lengths[0], G)
    cos_tab, sine_tab = rope_tables(positions, HEAD)
    xa = x_all.astype(F32)
    normed = (xa * rms_scale(xa) * gain_attn).astype(BF)
    qkv = dot_nn(normed, w_all)
    queries = qkv[:, :qw].reshape(G, hl, HEAD)
    keys_raw = qkv[:, qw : qw + kw].reshape(G, kl, HEAD)
    v_kv = qkv[:, qw + kw :].astype(BF).reshape(G, kl, HEAD)
    inv_query = rms_scale(queries)
    q_local = rotate(queries * inv_query * gain_query, cos_tab, sine_tab).astype(BF)
    inv_key = rms_scale(keys_raw)
    k_kv = rotate(keys_raw * inv_key * gain_key, cos_tab, sine_tab).astype(BF)
    k_local = jnp.repeat(k_kv, share, axis=1)
    v_local = jnp.repeat(v_kv, share, axis=1)
    token = jnp.arange(G, dtype=jnp.int32)
    allowed = (segment[:, None] == segment[None, :]) & (token[None, :] <= token[:, None])
    scores = (
        jnp.einsum("qhd,khd->hqk", q_local, k_local, preferred_element_type=F32) * scale_att
    )
    scores = jnp.where(allowed[None], scores, masked_score)
    top = jnp.max(scores, axis=2, keepdims=True)
    log_total = top + jnp.log(jnp.sum(jnp.exp(scores - top), axis=2, keepdims=True))
    prob_full = jnp.exp(scores - log_total)
    prob_bf = prob_full.astype(BF)
    o_local = jnp.einsum("hqk,khd->qhd", prob_bf, v_local, preferred_element_type=F32).astype(BF)
    o_flat = o_local.reshape(G, qw)
    part = dot_nn(o_flat, wo).astype(BF).reshape(CL, CD, T, W)
    dy_all, attn_sum = communicate(
        [Gather("fsdp", (T, W), BF, "both"), Reduce("ctx", (T, W), BF, 2)],
        [out_cotangent, part],
        2,
    )
    dy_all = dy_all.reshape(F * T, W)

    x_float = block_input.astype(F32)
    inv_one = rms_scale(x_float)
    mixed_res = x_float + attn_sum
    inv_two = rms_scale(mixed_res)
    ffn_in = (mixed_res * inv_two * gain_ffn).astype(BF)
    (ffn_all,) = communicate([Gather("fsdp", (T, W), BF, "both")], [ffn_in], 3)
    ffn_all = ffn_all.reshape(F * T, W)
    gate_pre = dot_nt(ffn_all, gate_proj)
    up_pre = dot_nt(ffn_all, up_proj)
    gate_sig = jax.nn.sigmoid(gate_pre)
    active = gate_pre * gate_sig
    hidden = (active * up_pre).astype(BF)
    d_hidden = dot_nt(dy_all, down_proj)
    d_gate = (d_hidden * up_pre * gate_sig * (1.0 + gate_pre * (1.0 - gate_sig))).astype(BF)
    d_up = (d_hidden * active).astype(BF)
    ffc = gate_proj.shape[0] // C
    grads = [
        dot_tn(a, b).astype(BF).reshape(CL, CD, ffc, W)
        for a, b in ((d_gate, ffn_all), (d_up, ffn_all), (hidden, dy_all))
    ]
    down_part = dot_nn(hidden, down_proj).astype(BF).reshape(L, D, T, W)
    back_part = (
        (dot_nn(d_gate, gate_proj) + dot_nn(d_up, up_proj)).astype(BF).reshape(L, D, T, W)
    )
    gate_grad, d_ffn_in, ffn_out = communicate(
        [
            Reduce("ctx", (ffc, W), BF),
            Reduce("fsdp", (T, W), BF, 4, 1),
            Reduce("fsdp", (T, W), BF, 4, 1),
        ],
        grads[:1] + [back_part, down_part],
        4,
    )
    block_output = (mixed_res + ffn_out).astype(BF)
    grad_gain_ffn = jnp.sum(d_ffn_in * mixed_res * inv_two, axis=0)
    d_mixed = out_cotangent.astype(F32) + norm_back(mixed_res, inv_two, gain_ffn, d_ffn_in)
    (dm_all,) = communicate([Gather("ctx", (T, W), BF, "line")], [d_mixed.astype(BF)], 5)
    dm_all = dm_all.reshape(G, W)
    d_local = dot_nt(dm_all, wo).astype(BF).reshape(G, hl, HEAD)
    row_delta = jnp.sum(d_local.astype(F32) * o_local.astype(F32), axis=2).T[:, :, None]
    d_prob = jnp.einsum("qhd,khd->hqk", d_local, v_local, preferred_element_type=F32)
    d_score = (prob_full * (d_prob - row_delta) * scale_att).astype(BF)
    dq_rot = jnp.einsum("hqk,khd->qhd", d_score, k_local, preferred_element_type=F32).astype(BF)
    dk_sum = jnp.einsum("hqk,qhd->khd", d_score, q_local, preferred_element_type=F32)
    dv_sum = jnp.einsum("hqk,qhd->khd", prob_bf, d_local, preferred_element_type=F32)
    dk_rot = jnp.sum(dk_sum.reshape(G, kl, share, HEAD), axis=2).astype(BF)
    d_values = jnp.sum(dv_sum.reshape(G, kl, share, HEAD), axis=2).astype(BF)
    d_q_norm = unrotate(dq_rot.astype(F32), cos_tab, sine_tab)
    d_k_norm = unrotate(dk_rot.astype(F32), cos_tab, sine_tab)
    grad_gain_q = jnp.sum(d_q_norm * queries * inv_query, axis=(0, 1))
    grad_gain_k = jnp.sum(d_k_norm * keys_raw * inv_key, axis=(0, 1))
    d_queries = norm_back(queries, inv_query, gain_query, d_q_norm).astype(BF).reshape(G, qw)
    d_keys = norm_back(keys_raw, inv_key, gain_key, d_k_norm).astype(BF).reshape(G, kw)
    d_qkv = jnp.concatenate([d_queries, d_keys, d_values.reshape(G, kw)], axis=1)
    dn_part = dot_nt(d_qkv, w_all).astype(BF).reshape(CL, CD, T, W)
    qkv_part = dot_tn(normed, d_qkv).astype(BF).reshape(L, D, rows, qw + 2 * kw)
    wo_part = dot_tn(o_flat, dm_all).astype(BF).reshape(L, D, qw // F, W)
    d_normed, qkv_sum, wo_sum, up_grad, down_grad = communicate(
        [
            Reduce("ctx", (T, W), BF),
            Reduce("fsdp", qkv_part.shape[2:], BF, 2, 1, 0, BF),
            Reduce("fsdp", wo_part.shape[2:], BF, 1, 0, 0, BF),
            Reduce("ctx", (ffc, W), BF),
            Reduce("ctx", (ffc, W), BF),
        ],
        [dn_part, qkv_part, wo_part] + grads[1:],
        6,
    )
    grad_gain_attn = jnp.sum(d_normed * x_float * inv_one, axis=0)
    input_grad = d_mixed + norm_back(x_float, inv_one, gain_attn, d_normed)
    pair = jnp.concatenate([grad_gain_q, grad_gain_k])
    gains = jnp.concatenate(
        [
            jnp.pad(vec.reshape(F, 1, -1), ((0, 0), (0, 0), (0, 128 - vec.shape[0] // F)))
            for vec in (grad_gain_attn, grad_gain_ffn, pair)
        ]
        + [jnp.zeros((F, 5, 128), F32)],
        axis=1,
    )
    g_sum, query_grad, key_grad, value_grad, out_proj_grad = finish(
        gains, qkv_sum.reshape(C, rows // C, qw + 2 * kw), wo_sum, qw, kw, 7
    )
    query_grad, key_grad, value_grad, out_proj_grad, gate_grad, up_grad, down_grad = emit(
        [query_grad, key_grad, value_grad, out_proj_grad, gate_grad, up_grad, down_grad]
    )
    return (
        block_output,
        input_grad,
        g_sum[0, :gain_w],
        query_grad,
        key_grad,
        value_grad,
        g_sum[2, :pair_w],
        out_proj_grad,
        g_sum[1, :gain_w],
        gate_grad,
        up_grad,
        down_grad,
    )


def solution(mesh):
    return jax.shard_map(
        on_device,
        mesh=mesh,
        in_specs=(
            P(("fsdp", "ctx"), None),
            P("fsdp"),
            P("fsdp", None),
            P("fsdp", None),
            P("fsdp", None),
            P("fsdp"),
            P("fsdp", None),
            P("fsdp"),
            P("fsdp", None),
            P("fsdp", None),
            P("fsdp", None),
            P("fsdp", None),
            P(("fsdp", "ctx"), None),
        ),
        out_specs=(
            P(("fsdp", "ctx"), None),
            P(("fsdp", "ctx"), None),
            P("fsdp"),
            P(("fsdp", "ctx"), None),
            P(("fsdp", "ctx"), None),
            P(("fsdp", "ctx"), None),
            P("fsdp"),
            P(("fsdp", "ctx"), None),
            P("fsdp"),
            P(("fsdp", "ctx"), None),
            P(("fsdp", "ctx"), None),
            P(("fsdp", "ctx"), None),
        ),
        check_vma=False,
    )
```
